32 devices in a mesh: row: 2 (over x), col: 16 (over z, y, core).
Axes of the slice: x: 2, y: 2, z: 4, core: 2. Of those that a mesh axis runs over, the one named last changes fastest.
Arguments:
- query_proj: bfloat16 [16384, 4096], P(('col', 'row')), may hold values from -9 to 9
- key_proj: bfloat16 [16384, 512], P(('col', 'row')), may hold values from -9 to 9
- value_proj: bfloat16 [16384, 512], P(('col', 'row')), may hold values from -6 to 6
- segment_ids: int32 [16, 1024], P('col'), may hold values from 0 to 3, never falling along the last dimension, each value on 1 to 512 neighbouring positions
- out_weight: bfloat16 [4096, 8192], P('col', 'row'), may hold values from -0.09375 to 0.09375
- residual: bfloat16 [16384, 8192], P('col', 'row'), may hold values from -4 to 4
- norm_gain: float32 [8192], P('row'), may hold values from 0.1 to 1.9
Outputs:
- residual_sum: bfloat16 [16384, 8192], P('col', 'row')
- normed: bfloat16 [16384, 8192], P('col', 'row')
The draws below stay inside these ranges and needn't reach their ends.
Inputs may be any that keep to these rules, and one draw needn't show every extreme that they name: `segment_ids`: along each packed sequence the document number never falls; each document spans at most 512 positions and one spans exactly that.
All inputs are finite; a program needn't handle non-finite values.
Results may differ from the reference program's by a relative error of at most 0.0044.
Values may be sent and summed in bfloat16 or wider, within the bound.
A program may use at most 192 MiB of HBM per device.

```python
import math
import jax
import jax.numpy as jnp
import numpy as np
from jax import lax

D = 8192
HD = 128
HQ = 32
HK = 4
SEQ = 1024
QW = 4096
PACKS = 16
TOKENS = 16384


def shared_keys(key):
    width = HK * HD
    base_keys = jnp.clip(jax.random.normal(jax.random.fold_in(key, 11), (TOKENS, width), jnp.float32), -4.0, 4.0)
    keys_out = base_keys
    return keys_out


def draw_key_proj(key, part):
    keys_out = shared_keys(key)
    return keys_out.astype(jnp.bfloat16)


def draw_query_proj(key, part):
    query_out = jnp.clip(jax.random.normal(jax.random.fold_in(key, 21), (TOKENS, HQ * HD), jnp.float32), -4.0, 4.0)
    return query_out.astype(jnp.bfloat16)


def block_levels(stream_key, shape, split, low, largest):
    factor_of, own = 1.0, jax.random.fold_in(stream_key, 6)
    for axis_at, parts in split:
        steps = jnp.exp(jax.random.uniform(jax.random.fold_in(own, axis_at), (parts,), jnp.float32, low / len(split), largest / len(split)))
        factor_of = factor_of * jnp.repeat(steps, shape[axis_at] // parts).reshape([-1 if axis == axis_at else 1 for axis in range(len(shape))])
    return factor_of


def length_profile(amount, total, limit, skew):
    weights = [(1 << 20) // math.isqrt(grade ** skew) + 1 for grade in range(2, amount + 1)]
    rest, given = total - limit - (amount - 1), [1] * (amount - 1)
    while rest > 0:
        free = [i for i in range(amount - 1) if given[i] < limit]
        pool, remaining = sum([weights[i] for i in free]), rest
        for i in free:
            extra = min(limit - given[i], max(1, remaining * weights[i] // pool), rest)
            given[i] = given[i] + extra
            rest = rest - extra
    return np.array([limit] + given)


def ragged_sizes(key, number_of, total, reach, slope):
    if number_of == 2:
        one = jax.random.randint(key, (), max(1, total - reach), min(reach, total - 1) + 1)
        return jnp.stack([one, total - one])
    sizes = jnp.asarray(length_profile(number_of, total, reach, slope), jnp.int32)
    couples = (number_of - 1) // 2
    donor, receiver = sizes[1:1 + 2 * couples:2], sizes[2:2 + 2 * couples:2]
    slack = jnp.minimum(donor - 1, reach - receiver)
    moved = jax.random.randint(jax.random.fold_in(key, 1), (couples,), 0, 1 << 20) % (slack + 1)
    sizes = sizes.at[1:1 + 2 * couples:2].set(donor - moved).at[2:2 + 2 * couples:2].set(receiver + moved)
    return sizes[jax.random.permutation(jax.random.fold_in(key, 2), number_of)]


def noise(rng, dims, scale, limit, pieces=(), held_as=jnp.bfloat16):
    values = scale * jax.random.normal(rng, dims, jnp.float32)
    if pieces:
        values = values * block_levels(rng, dims, pieces, -0.22, 0.18)
    return jnp.clip(values, -limit, limit).astype(held_as)


def setup_inputs(seed: int = 0) -> dict:
    keys = jax.random.split(jax.random.key(seed), 8)
    query_proj = draw_query_proj(jax.random.fold_in(keys[7], 71), 0)
    key_proj = draw_key_proj(jax.random.fold_in(keys[7], 71), 0)
    value_proj = noise(keys[2], (TOKENS, HK * HD), 1.0, 6.0, ((0, 32),))
    segment_ids = jax.vmap(lambda own: jnp.searchsorted(jnp.cumsum(ragged_sizes(own, 4, SEQ, SEQ // 2, 0)), jnp.arange(SEQ), side="right"))(jax.random.split(keys[3], PACKS)).reshape((PACKS, SEQ)).astype(jnp.int32)
    out_weight = noise(keys[4], (QW, D), QW ** -0.5, 0.09375, ((0, 16), (1, 2)))
    residual = noise(keys[5], (TOKENS, D), 0.25, 4.0, ((0, 16), (1, 2)))
    norm_gain = jnp.clip(1.0 + 0.18 * jax.random.normal(keys[6], (D,), jnp.float32), 0.1, 1.9)
    return {"query_proj": query_proj, "key_proj": key_proj, "value_proj": value_proj, "segment_ids": segment_ids, "out_weight": out_weight, "residual": residual, "norm_gain": norm_gain}


def attend_pack(operands):
    query_rows, key_rows, value_rows, segment_row = operands
    group = HQ // HK
    query_grid = query_rows.reshape(SEQ, HK, group, HD).transpose(1, 2, 0, 3).astype(jnp.float32)
    key_grid = key_rows.reshape(SEQ, HK, HD).transpose(1, 0, 2).astype(jnp.float32)
    value_grid = value_rows.reshape(SEQ, HK, HD).transpose(1, 0, 2).astype(jnp.float32)
    places = jnp.arange(SEQ)
    allowed = (segment_row[:, None] == segment_row[None, :]) & (places[None, :] <= places[:, None])
    scores = jnp.einsum('hgqd,hkd->hgqk', query_grid, key_grid) * HD ** (-0.5)
    scores = jnp.where(allowed, scores, jnp.float32(-1e+30))
    peak = lax.optimization_barrier(jnp.max(scores, axis=-1, keepdims=True))
    weights = jnp.where(allowed, jnp.exp(scores - peak), jnp.float32(0.0))
    totals = lax.optimization_barrier(jnp.sum(weights, axis=-1, keepdims=True))
    probs = lax.optimization_barrier(weights.astype(jnp.bfloat16))
    mixture = jnp.einsum('hgqk,hkd->hgqd', probs.astype(jnp.float32), value_grid) / totals
    mixture = mixture.astype(jnp.bfloat16)
    return mixture.transpose(2, 0, 1, 3).reshape(SEQ, HQ * HD)

def reference(query_proj, key_proj, value_proj, segment_ids, out_weight, residual, norm_gain):
    packs = segment_ids.shape[0]
    query_all = query_proj.reshape(packs, SEQ, HQ * HD)
    key_all = key_proj.reshape(packs, SEQ, HK * HD)
    value_all = value_proj.reshape(packs, SEQ, HK * HD)
    attn = lax.map(attend_pack, (query_all, key_all, value_all, segment_ids))
    attn = attn.reshape(packs * SEQ, HQ * HD)
    projected = jnp.dot(attn, out_weight, preferred_element_type=jnp.float32)
    hidden_sum = residual.astype(jnp.float32) + projected
    mean_square = lax.optimization_barrier(jnp.mean(hidden_sum * hidden_sum, axis=1))
    scaled = lax.rsqrt(mean_square + jnp.float32(1e-05))
    normed = hidden_sum * scaled[:, None] * norm_gain[None, :]
    return (hidden_sum.astype(jnp.bfloat16), normed.astype(jnp.bfloat16))
```

```python
import functools
import math

import jax
import jax.numpy as jnp
from jax import lax
from jax.experimental import pallas as pl
from jax.experimental.pallas import tpu as pltpu
from jax.sharding import PartitionSpec as P

D = 8192
HD = 128
HK = 4
MESH = pl.DeviceIdType.MESH


def attend_local(query_heads, key_heads, value_heads, segment_row):
    length = query_heads.shape[0]
    kv_local = key_heads.shape[1] // HD
    group = query_heads.shape[1] // HD // kv_local
    query_grid = query_heads.reshape(length, kv_local, group, HD).transpose(1, 2, 0, 3)
    key_grid = key_heads.reshape(length, kv_local, HD).transpose(1, 0, 2)
    value_grid = value_heads.reshape(length, kv_local, HD).transpose(1, 0, 2)
    places = jnp.arange(length)
    allowed = (segment_row[:, None] == segment_row[None, :]) & (places[None, :] <= places[:, None])

    def one_group(operands):
        group_query, group_key, group_value = operands
        scores = jnp.einsum(
            "gqd,kd->gqk", group_query, group_key, preferred_element_type=jnp.float32
        ) * HD ** (-0.5)
        scores = jnp.where(allowed, scores, jnp.float32(-1e30))
        peak = jnp.max(scores, axis=-1, keepdims=True)
        weights = jnp.where(allowed, jnp.exp(scores - peak), jnp.float32(0.0))
        totals = jnp.sum(weights, axis=-1, keepdims=True)
        probs = weights.astype(jnp.bfloat16)
        mixture = (
            jnp.einsum("gqk,kd->gqd", probs, group_value, preferred_element_type=jnp.float32)
            / totals
        )
        return mixture.astype(jnp.bfloat16)

    heads_out = lax.map(one_group, (query_grid, key_grid, value_grid))
    return heads_out.transpose(2, 0, 1, 3).reshape(length, kv_local * group * HD)


def widen_heads(proj_rows, repeat):
    rows_local = proj_rows.shape[0]
    kv_count = proj_rows.shape[1] // HD
    if repeat == 1:
        return proj_rows
    spread = jnp.broadcast_to(
        proj_rows.reshape(rows_local, kv_count, 1, HD), (rows_local, kv_count, repeat, HD)
    )
    return spread.reshape(rows_local, kv_count * repeat * HD)


def body_any(query_proj, key_proj, value_proj, segment_ids, out_weight, residual, norm_gain):
    row_count = lax.axis_size("row")
    repeat = max(row_count // HK, 1)
    key_wide = widen_heads(key_proj, repeat)
    value_wide = widen_heads(value_proj, repeat)
    query_heads, key_heads, value_heads = (
        lax.all_to_all(query_proj, "row", split_axis=1, concat_axis=0, tiled=True),
        lax.all_to_all(key_wide, "row", split_axis=1, concat_axis=0, tiled=True),
        lax.all_to_all(value_wide, "row", split_axis=1, concat_axis=0, tiled=True),
    )
    attn = attend_local(query_heads, key_heads, value_heads, segment_ids[0])
    panel_rows = lax.all_gather(attn, "row", axis=1, tiled=True)
    projected = jnp.dot(
        panel_rows,
        lax.all_gather(out_weight, "col", axis=0, tiled=True),
        preferred_element_type=jnp.float32,
    )
    hidden_sum = residual.astype(jnp.float32) + projected
    squares = lax.psum(jnp.sum(hidden_sum * hidden_sum, axis=1), "row")
    scaled = lax.rsqrt(squares / D + jnp.float32(1e-05))
    normed = hidden_sum * scaled[:, None] * norm_gain[None, :]
    return (hidden_sum.astype(jnp.bfloat16), normed.astype(jnp.bfloat16))


NZ = 4
CH = 8
QT = 256
KT = 768
POS = 8
IN, OUT, ACROSS, SIB = range(4)


def fused_kernel(q_ref, k_ref, v_ref, seg_row, w_ref, res_ref,
                 acc, sq_ref,
                 wfull, kvbuf, bias, attn, part, sqbuf,
                 send, recv, loc, rsem, a_send, a_recv, kv_send, kv_recv, x_send, x_recv):
    r = lax.axis_index("row")
    col = lax.axis_index("col")
    core = lax.rem(col, 2)
    y = lax.rem(col // 2, 2)
    z = col // 4
    half = q_ref.shape[0]
    wrows, width = w_ref.shape
    cw = width // CH
    aw = q_ref.shape[1] // POS

    end = 1 - (z * (3 - z)) // 2
    step = 1 - 2 * (z // 2)
    planes = (z, z + step * (2 * end - 1), z + step * (1 + end), z + step * (2 + end))
    is_end = end == 1
    is_mid = end == 0

    def cid(zz, yy, cc):
        return (zz * 2 + yy) * 2 + cc

    inner = (r, cid(z + step, y, core))
    outer = (r, cid(z - step, y, core))
    across = (r, cid(z, 1 - y, core))
    sibling = (r, cid(z, y, 1 - core))
    partner = (1 - r, col)
    devices = (inner, outer, across, sibling)

    def unit(pos):
        return planes[pos // 2] * 2 + (y if pos % 2 == 0 else 1 - y)

    units = [unit(pos) for pos in range(POS)]

    def unit_at(g):
        h = g // 2
        plane = planes[0] + (h == 1) * (planes[1] - planes[0])
        plane = plane + (h == 2) * (planes[2] - planes[0])
        plane = plane + (h == 3) * (planes[3] - planes[0])
        odd = lax.rem(g, 2)
        return plane * 2 + y + odd * (1 - 2 * y), plane

    barrier = pltpu.get_barrier_semaphore()

    def greet(dev):
        pl.semaphore_signal(barrier, inc=1, device_id=dev, device_id_type=MESH)

    greet(inner)
    greet(across)
    greet(sibling)
    greet(partner)

    @pl.when(is_mid)
    def _():
        greet(outer)

    kbuf, vbuf, rbuf = kvbuf.at[0], kvbuf.at[1], kvbuf

    own_rows = pl.ds(pl.multiple_of(r * half, half), half)
    own_w = pltpu.make_async_copy(
        w_ref, wfull.at[units[0], pl.ds(pl.multiple_of(core * wrows, wrows), wrows), :], loc.at[0])
    k_local = pltpu.make_async_copy(k_ref, kbuf.at[own_rows, :], loc.at[1])
    v_local = pltpu.make_async_copy(v_ref, vbuf.at[own_rows, :], loc.at[2])
    q_local = pltpu.make_async_copy(q_ref, attn.at[own_rows, :], loc.at[3])
    q_local.start()
    k_local.start()
    v_local.start()

    @pl.when(is_end)
    def _():
        pl.semaphore_wait(barrier, 4)

    @pl.when(is_mid)
    def _():
        pl.semaphore_wait(barrier, 5)

    def cols_of(j):
        return pl.ds(pl.multiple_of(j * cw, cw), cw)

    def chunk(u, c, j):
        return wfull.at[u, pl.ds(pl.multiple_of(c * wrows, wrows), wrows), cols_of(j)]

    def xfer(way, u, j, own=False):
        dst = chunk(u, core, j)
        return pltpu.make_async_remote_copy(
            src_ref=w_ref.at[:, cols_of(j)] if own else dst, dst_ref=dst,
            send_sem=send.at[way, u, j], recv_sem=recv.at[u, core, j],
            device_id=devices[way], device_id_type=MESH)

    def arrived(u, c, j):
        ref = chunk(u, c, j)
        pltpu.make_async_copy(ref, ref, recv.at[u, c, j]).wait()

    def kv_remote(h, i):
        cols = pl.ds(pl.multiple_of(h * HD, HD), HD)
        src, dst = ((k_ref, kbuf), (v_ref, vbuf))[i]
        return pltpu.make_async_remote_copy(
            src_ref=src.at[:, cols], dst_ref=dst.at[pl.ds(0, half), cols],
            send_sem=kv_send.at[i, h], recv_sem=kv_recv.at[i, h],
            device_id=partner, device_id_type=MESH)

    @pl.when(r == 0)
    def _():
        for plane in planes:
            kv_remote(plane, 0).start()
            kv_remote(plane, 1).start()

    @pl.loop(0, CH)
    def _(j):
        xfer(IN, units[0], j, True).start()

        @pl.when(is_mid)
        def _():
            xfer(OUT, units[0], j, True).start()

        xfer(ACROSS, units[0], j, True).start()

    @pl.loop(0, CH)
    def _(j):
        xfer(SIB, units[0], j, True).start()

    own_w.start()

    def res_copy(j):
        return pltpu.make_async_copy(res_ref.at[:, cols_of(j)], rbuf.at[lax.rem(j, 2)],
                                     rsem.at[lax.rem(j, 2)])

    def mask(i, t0, ks, kt):
        qrow = seg_row[:, t0:t0 + QT].astype(jnp.float32)
        qs = jnp.broadcast_to(qrow, (128, QT)).T[:, :1]
        ksg = seg_row[:, ks:ks + kt].astype(jnp.float32)
        qp = t0 + lax.broadcasted_iota(jnp.int32, (QT, kt), 0)
        kp = ks + lax.broadcasted_iota(jnp.int32, (QT, kt), 1)
        keep = (qs == ksg) & (kp <= qp)
        bias[i, :, :kt] = jnp.where(keep, jnp.float32(0.0), jnp.float32(-1e30))

    def windows(row):
        out = []
        for i in range(half // QT):
            t0 = row * half + i * QT
            ks = max(t0 + QT - KT, 0)
            out.append((i, t0, ks, t0 + QT - ks))
        return out

    for row in range(2):
        @pl.when(r == row)
        def _():
            for w in windows(row):
                mask(*w)

    q_local.wait()
    k_local.wait()
    v_local.wait()

    scale = HD ** (-0.5) * math.log2(math.e)

    def attend(u, plane, row):
        kcol = pl.ds(pl.multiple_of(plane * HD, HD), HD)
        for i, t0, ks, kt in windows(row):
            key = kbuf[ks:ks + kt, kcol]
            val = vbuf[ks:ks + kt, kcol]
            for h in range(aw // HD):
                hc = pl.ds(pl.multiple_of(u * aw + h * HD, HD), HD)
                s = lax.dot_general(attn[t0:t0 + QT, hc], key, (((1,), (1,)), ((), ())),
                                    preferred_element_type=jnp.float32)
                s = s * scale + bias[i, :, :kt]
                m = jnp.max(s, axis=1, keepdims=True)
                p = jnp.exp2(s - m)
                tot = jnp.sum(p, axis=1, keepdims=True)
                o = jnp.dot(p.astype(jnp.bfloat16), val, preferred_element_type=jnp.float32)
                attn[t0:t0 + QT, hc] = (o / tot).astype(jnp.bfloat16)

    def attn_copy(u, rows):
        ref = attn.at[rows, pl.ds(pl.multiple_of(u * aw, aw), aw)]
        return pltpu.make_async_remote_copy(
            src_ref=ref, dst_ref=ref, send_sem=a_send.at[u], recv_sem=a_recv.at[u],
            device_id=partner, device_id_type=MESH)

    other_rows = pl.ds(pl.multiple_of((1 - r) * half, half), half)

    def attn_arrived(u):
        ref = attn.at[other_rows, pl.ds(pl.multiple_of(u * aw, aw), aw)]
        pltpu.make_async_copy(ref, ref, a_recv.at[u]).wait()

    def take(u, j, *ways):
        arrived(u, core, j)
        for way in ways:
            xfer(way, u, j).start()
        xfer(SIB, u, j).start()

    @pl.loop(0, POS)
    def _(g):
        u, plane = unit_at(g)

        @pl.when((r == 1) & (lax.rem(g, 2) == 0))
        def _():
            kv_remote(plane, 0).wait_recv()
            kv_remote(plane, 1).wait_recv()

        for row in range(2):
            @pl.when(r == row)
            def _():
                attend(u, plane, row)

        attn_copy(u, own_rows).start()

        @pl.when(is_end)
        def _():
            take(units[1], g, IN)
            arrived(units[2], core, g)

            @pl.when(g < CH // 2)
            def _():
                xfer(ACROSS, units[2], g).start()

            xfer(SIB, units[2], g).start()

        @pl.when(is_mid)
        def _():
            take(units[4], g, OUT, ACROSS)
            take(units[2], g, IN)
            take(units[1], g)

    def product(pos, cols):
        u = units[pos]
        return jnp.dot(attn[:, pl.ds(pl.multiple_of(u * aw, aw), aw)], wfull[u, :, cols],
                       preferred_element_type=jnp.float32)

    def add(j, *positions):
        for pos in positions:
            arrived(units[pos], 1 - core, j)
        cols = cols_of(j)
        for pos in positions:
            acc[:, cols] += product(pos, cols)

    def square(j):
        sqr = None
        for i in range(cw // 128):
            a = acc[:, pl.ds(pl.multiple_of(j * cw + i * 128, 128), 128)]
            sqr = a * a if sqr is None else sqr + a * a
        part[...] += sqr

    hc = CH // 2
    res_copy(0).start()
    part[...] = jnp.zeros_like(part)
    own_w.wait()

    @pl.loop(0, CH)
    def _(j):
        @pl.when(is_end)
        def _():
            take(units[4], j, ACROSS)
            late = (j >= hc) * 1
            take(units[3] + late * (units[5] - units[3]), j - late * hc)

        @pl.when(is_mid)
        def _():
            take(units[6], j, OUT, ACROSS)
            take(units[3], j)
            take(units[5], j)

        @pl.when(j == 0)
        def _():
            for pos in range(3):
                attn_arrived(units[pos])

        @pl.when(j < CH - 1)
        def _():
            res_copy(j + 1).start()

        res_copy(j).wait()
        acc[:, cols_of(j)] = rbuf[lax.rem(j, 2)].astype(jnp.float32)
        add(j, 0, 1, 2)

    @pl.loop(0, hc)
    def _(j):
        @pl.when(is_end)
        def _():
            take(units[6], j, ACROSS)
            take(units[5], j + hc)

        @pl.when(is_mid)
        def _():
            xfer(OUT, units[1], j + hc).start()
            take(units[7], j)

        @pl.when(j == 0)
        def _():
            for pos in range(3, 6):
                attn_arrived(units[pos])

        add(j, 3, 4, 5)

    @pl.loop(0, hc)
    def _(j):
        @pl.when(is_end)
        def _():
            take(units[6], j + hc, ACROSS)
            take(units[7], j)

        @pl.when(is_mid)
        def _():
            take(units[7], j + hc)

        @pl.when(j == 0)
        def _():
            for pos in range(6, 8):
                attn_arrived(units[pos])

        add(j + hc, 4, 5)
        add(j, 6, 7)
        square(j)

    def sent(way, pos, j):
        xfer(way, units[pos], j).wait_send()

    @pl.loop(0, hc)
    def _(i):
        j = i + hc
        add(j, 6)
        for e in range(2):
            jj = 2 * i + e
            sent(IN, 0, jj)
            sent(ACROSS, 0, jj)
            sent(ACROSS, 4, jj)
            for pos in (0, 1, 2, 4):
                sent(SIB, pos, jj)

            @pl.when(is_end)
            def _():
                sent(IN, 1, jj)

            @pl.when(is_mid)
            def _():
                sent(IN, 2, jj)
                sent(OUT, 0, jj)
                sent(OUT, 4, jj)

        @pl.when(is_end)
        def _():
            take(units[3], j)
            take(units[7], j)

        add(j, 3, 7)
        square(j)

    sqbuf[0] = jnp.sum(part[...].T, axis=0, keepdims=True)
    x_sq = pltpu.make_async_remote_copy(
        src_ref=sqbuf.at[0], dst_ref=sqbuf.at[1], send_sem=x_send.at[0], recv_sem=x_recv.at[0],
        device_id=partner, device_id_type=MESH)
    x_sq.start()

    @pl.when(r == 0)
    def _():
        for plane in planes:
            kv_remote(plane, 0).wait_send()
            kv_remote(plane, 1).wait_send()

    @pl.loop(0, POS)
    def _(u):
        attn_copy(u, own_rows).wait_send()

    @pl.loop(0, CH)
    def _(j):
        sent(ACROSS, 6, j)
        for pos in (3, 5, 6, 7):
            sent(SIB, pos, j)

        @pl.when(is_mid)
        def _():
            sent(OUT, 6, j)

        @pl.when(is_end & (j < hc))
        def _():
            sent(ACROSS, 2, j)

        @pl.when(is_mid & (j >= hc))
        def _():
            sent(OUT, 1, j)

    x_sq.wait()
    sq_ref[...] = sqbuf[0] + sqbuf[1]


NR = 128


def norm_kernel(acc, sq_ref, gain_ref, sum_ref, out_ref, hbuf, nbuf, hsem, nsem):
    rows = acc.shape[0]

    def copies(i):
        block = pl.ds(pl.multiple_of(i * NR, NR), NR)
        return (pltpu.make_async_copy(hbuf.at[block, :], sum_ref.at[block, :], hsem.at[i]),
                pltpu.make_async_copy(nbuf.at[block, :], out_ref.at[block, :], nsem.at[i]))

    @pl.loop(0, rows // NR)
    def _(i):
        block = pl.ds(pl.multiple_of(i * NR, NR), NR)
        scaled = lax.rsqrt(sq_ref[:, block] / D + jnp.float32(1e-05))
        column = jnp.broadcast_to(scaled, (128, NR)).T[:, :1]
        for n in range(acc.shape[1] // 512):
            cols = slice(n * 512, (n + 1) * 512)
            hid = acc[block, cols]
            hbuf[block, cols] = hid.astype(jnp.bfloat16)
            nbuf[block, cols] = (hid * column * gain_ref[:, cols]).astype(jnp.bfloat16)
        for c in copies(i):
            c.start()

    @pl.loop(0, rows // NR)
    def _(i):
        for c in copies(i):
            c.wait()


def body_fused(query_proj, key_proj, value_proj, segment_ids, out_weight, residual, norm_gain):
    half, qw = query_proj.shape
    length = segment_ids.shape[1]
    wrows, width = out_weight.shape
    hbm = pl.BlockSpec(memory_space=pl.ANY)
    vmem = pl.BlockSpec(memory_space=pltpu.VMEM)
    dma = pltpu.SemaphoreType.DMA
    total, squares = pl.pallas_call(
        fused_kernel,
        out_shape=(
            pltpu.VMEM((length, width), jnp.float32),
            pltpu.VMEM((1, length), jnp.float32),
        ),
        in_specs=[hbm, hbm, hbm, vmem, hbm, hbm],
        out_specs=(vmem, vmem),
        scratch_shapes=[
            pltpu.VMEM((POS, 2 * wrows, width), jnp.bfloat16),
            pltpu.VMEM((2, length, HK * HD), jnp.bfloat16),
            pltpu.VMEM((half // QT, QT, KT), jnp.float32),
            pltpu.VMEM((length, qw), jnp.bfloat16),
            pltpu.VMEM((length, 128), jnp.float32),
            pltpu.VMEM((2, 1, length), jnp.float32),
            dma((4, POS, CH)),
            dma((POS, 2, CH)),
            dma((4,)),
            dma((2,)),
            dma((POS,)),
            dma((POS,)),
            dma((2, HK)),
            dma((2, HK)),
            dma((1,)),
            dma((1,)),
        ],
        compiler_params=pltpu.CompilerParams(
            collective_id=0, has_side_effects=True, vmem_limit_bytes=(47 * 1024 + 768) * 1024),
        name="fused",
    )(query_proj, key_proj, value_proj, segment_ids,
      out_weight, residual)
    total = pltpu.with_memory_space_constraint(total, pltpu.VMEM)
    squares = pltpu.with_memory_space_constraint(squares, pltpu.VMEM)
    return tuple(pl.pallas_call(
        norm_kernel,
        out_shape=(jax.ShapeDtypeStruct((length, width), jnp.bfloat16),) * 2,
        in_specs=[vmem, vmem, vmem],
        out_specs=(hbm, hbm),
        scratch_shapes=[
            pltpu.VMEM((length, width), jnp.bfloat16),
            pltpu.VMEM((length, width), jnp.bfloat16),
            dma((length // NR,)),
            dma((length // NR,)),
        ],
        compiler_params=pltpu.CompilerParams(vmem_limit_bytes=24 * 1024 * 1024),
        name="norm",
    )(total, squares, norm_gain.reshape(1, width)))


def solution(mesh):
    placed = (
        P(("col", "row"), None),
        P(("col", "row"), None),
        P(("col", "row"), None),
        P("col", None),
        P("col", "row"),
        P("col", "row"),
        P("row"),
    )
    known = mesh.shape["row"] == 2 and mesh.shape["col"] == 4 * NZ
    return jax.shard_map(
        body_fused if known else body_any,
        mesh=mesh,
        in_specs=placed,
        out_specs=(P("col", "row"), P("col", "row")),
        check_vma=False,
    )
```

```python
import functools
import math

import jax
import jax.numpy as jnp
from jax import lax
from jax.experimental import pallas as pl
from jax.experimental.pallas import tpu as pltpu
from jax.sharding import PartitionSpec as P

D = 8192
HD = 128
HK = 4
MESH = pl.DeviceIdType.MESH


def attend_local(query_heads, key_heads, value_heads, segment_row):
    length = query_heads.shape[0]
    kv_local = key_heads.shape[1] // HD
    group = query_heads.shape[1] // HD // kv_local
    query_grid = query_heads.reshape(length, kv_local, group, HD).transpose(1, 2, 0, 3)
    key_grid = key_heads.reshape(length, kv_local, HD).transpose(1, 0, 2)
    value_grid = value_heads.reshape(length, kv_local, HD).transpose(1, 0, 2)
    places = jnp.arange(length)
    allowed = (segment_row[:, None] == segment_row[None, :]) & (places[None, :] <= places[:, None])

    def one_group(operands):
        group_query, group_key, group_value = operands
        scores = jnp.einsum(
            "gqd,kd->gqk", group_query, group_key, preferred_element_type=jnp.float32
        ) * HD ** (-0.5)
        scores = jnp.where(allowed, scores, jnp.float32(-1e30))
        peak = jnp.max(scores, axis=-1, keepdims=True)
        weights = jnp.where(allowed, jnp.exp(scores - peak), jnp.float32(0.0))
        totals = jnp.sum(weights, axis=-1, keepdims=True)
        probs = weights.astype(jnp.bfloat16)
        mixture = (
            jnp.einsum("gqk,kd->gqd", probs, group_value, preferred_element_type=jnp.float32)
            / totals
        )
        return mixture.astype(jnp.bfloat16)

    heads_out = lax.map(one_group, (query_grid, key_grid, value_grid))
    return heads_out.transpose(2, 0, 1, 3).reshape(length, kv_local * group * HD)


def widen_heads(proj_rows, repeat):
    rows_local = proj_rows.shape[0]
    kv_count = proj_rows.shape[1] // HD
    if repeat == 1:
        return proj_rows
    spread = jnp.broadcast_to(
        proj_rows.reshape(rows_local, kv_count, 1, HD), (rows_local, kv_count, repeat, HD)
    )
    return spread.reshape(rows_local, kv_count * repeat * HD)


def body_any(query_proj, key_proj, value_proj, segment_ids, out_weight, residual, norm_gain):
    row_count = lax.axis_size("row")
    repeat = max(row_count // HK, 1)
    key_wide = widen_heads(key_proj, repeat)
    value_wide = widen_heads(value_proj, repeat)
    query_heads, key_heads, value_heads = (
        lax.all_to_all(query_proj, "row", split_axis=1, concat_axis=0, tiled=True),
        lax.all_to_all(key_wide, "row", split_axis=1, concat_axis=0, tiled=True),
        lax.all_to_all(value_wide, "row", split_axis=1, concat_axis=0, tiled=True),
    )
    attn = attend_local(query_heads, key_heads, value_heads, segment_ids[0])
    panel_rows = lax.all_gather(attn, "row", axis=1, tiled=True)
    projected = jnp.dot(
        panel_rows,
        lax.all_gather(out_weight, "col", axis=0, tiled=True),
        preferred_element_type=jnp.float32,
    )
    hidden_sum = residual.astype(jnp.float32) + projected
    squares = lax.psum(jnp.sum(hidden_sum * hidden_sum, axis=1), "row")
    scaled = lax.rsqrt(squares / D + jnp.float32(1e-05))
    normed = hidden_sum * scaled[:, None] * norm_gain[None, :]
    return (hidden_sum.astype(jnp.bfloat16), normed.astype(jnp.bfloat16))


NZ = 4
CH = 4
NC = 512
NS = 4
QT = 256
KT = 768
POS = 8
IN, OUT, ACROSS, SIB = range(4)


def fused_kernel(q_ref, k_ref, v_ref, seg_ref, w_ref, res_ref,
                 acc, sq_ref,
                 wfull, kvbuf, bias, attn, part, sqbuf, segbuf,
                 send, recv, t_send, t_recv, loc, wsem, rsem, a_send, a_recv, kv_send, kv_recv, x_send, x_recv):
    r = lax.axis_index("row")
    col = lax.axis_index("col")
    core = lax.rem(col, 2)
    y = lax.rem(col // 2, 2)
    z = col // 4
    half = q_ref.shape[0]
    wrows, width = w_ref.shape
    cw = width // CH
    aw = q_ref.shape[1] // POS

    end = 1 - (z * (3 - z)) // 2
    step = 1 - 2 * (z // 2)
    planes = (z, z + step * (2 * end - 1), z + step * (1 + end), z + step * (2 + end))
    is_end = end == 1
    is_mid = end == 0

    def cid(zz, yy, cc):
        return (zz * 2 + yy) * 2 + cc

    inner = (r, cid(z + step, y, core))
    outer = (r, cid(z - step, y, core))
    across = (r, cid(z, 1 - y, core))
    sibling = (r, cid(z, y, 1 - core))
    partner = (1 - r, col)
    devices = (inner, outer, across, sibling)

    def unit(pos):
        return planes[pos // 2] * 2 + (y if pos % 2 == 0 else 1 - y)

    units = [unit(pos) for pos in range(POS)]

    def unit_at(g):
        h = g // 2
        plane = planes[0] + (h == 1) * (planes[1] - planes[0])
        plane = plane + (h == 2) * (planes[2] - planes[0])
        plane = plane + (h == 3) * (planes[3] - planes[0])
        odd = lax.rem(g, 2)
        return plane * 2 + y + odd * (1 - 2 * y), plane

    barrier = pltpu.get_barrier_semaphore()

    def greet(dev):
        pl.semaphore_signal(barrier, inc=1, device_id=dev, device_id_type=MESH)

    greet(inner)
    greet(across)
    greet(sibling)
    greet(partner)

    @pl.when(is_mid)
    def _():
        greet(outer)

    kbuf, vbuf, rbuf = kvbuf.at[0], kvbuf.at[1], kvbuf

    own_rows = pl.ds(pl.multiple_of(r * half, half), half)
    k_local = pltpu.make_async_copy(k_ref, kbuf.at[own_rows, :], loc.at[0])
    v_local = pltpu.make_async_copy(v_ref, vbuf.at[own_rows, :], loc.at[1])
    q_local = pltpu.make_async_copy(q_ref, attn.at[own_rows, :], loc.at[2])
    seg_local = pltpu.make_async_copy(seg_ref, segbuf, loc.at[3])
    seg_local.start()
    q_local.start()
    k_local.start()
    v_local.start()

    @pl.when(is_end)
    def _():
        pl.semaphore_wait(barrier, 4)

    @pl.when(is_mid)
    def _():
        pl.semaphore_wait(barrier, 5)

    def cols_of(j):
        return pl.ds(pl.multiple_of(j * cw, cw), cw)

    def chunk(u, c, j):
        return wfull.at[u, j, pl.ds(pl.multiple_of(c * wrows, wrows), wrows), :]

    def own_copy(j):
        return pltpu.make_async_copy(w_ref.at[:, cols_of(j)], chunk(units[0], core, j), wsem.at[j])

    def xfer(way, u, j, own=False):
        dst = chunk(u, core, j)
        return pltpu.make_async_remote_copy(
            src_ref=w_ref.at[:, cols_of(j)] if own else dst, dst_ref=dst,
            send_sem=send.at[way, u, j], recv_sem=recv.at[u, core, j],
            device_id=devices[way], device_id_type=MESH)

    def arrived(u, c, j):
        ref = chunk(u, c, j)
        pltpu.make_async_copy(ref, ref, recv.at[u, c, j]).wait()

    def kv_remote(h, i):
        cols = pl.ds(pl.multiple_of(h * HD, HD), HD)
        src, dst = ((k_ref, kbuf), (v_ref, vbuf))[i]
        return pltpu.make_async_remote_copy(
            src_ref=src.at[:, cols], dst_ref=dst.at[pl.ds(0, half), cols],
            send_sem=kv_send.at[i, h], recv_sem=kv_recv.at[i, h],
            device_id=partner, device_id_type=MESH)

    @pl.loop(0, CH)
    def _(j):
        xfer(IN, units[0], j, True).start()

        @pl.when(is_mid)
        def _():
            xfer(OUT, units[0], j, True).start()

        xfer(ACROSS, units[0], j, True).start()

    @pl.when(r == 0)
    def _():
        for plane in planes:
            kv_remote(plane, 0).start()
            kv_remote(plane, 1).start()

    @pl.loop(0, CH)
    def _(j):
        xfer(SIB, units[0], j, True).start()
        own_copy(j).start()

    def part_cols(i):
        return pl.ds(pl.multiple_of(i * NC, NC), NC)

    def res_copy(i):
        slot = lax.rem(i, 2)
        return pltpu.make_async_copy(res_ref.at[:, part_cols(i)], rbuf.at[slot], rsem.at[slot])

    def mask(i, t0, ks, kt):
        qrow = segbuf[:, t0:t0 + QT].astype(jnp.float32)
        qs = jnp.broadcast_to(qrow, (128, QT)).T[:, :1]
        ksg = segbuf[:, ks:ks + kt].astype(jnp.float32)
        qp = t0 + lax.broadcasted_iota(jnp.int32, (QT, kt), 0)
        kp = ks + lax.broadcasted_iota(jnp.int32, (QT, kt), 1)
        keep = (qs == ksg) & (kp <= qp)
        bias[i, :, :kt] = jnp.where(keep, jnp.float32(0.0), jnp.float32(-1e30))

    def windows(row):
        out = []
        for i in range(half // QT):
            t0 = row * half + i * QT
            ks = max(t0 + QT - KT, 0)
            out.append((i, t0, ks, t0 + QT - ks))
        return out

    seg_local.wait()

    for row in range(2):
        @pl.when(r == row)
        def _():
            for w in windows(row):
                mask(*w)

    q_local.wait()
    k_local.wait()
    v_local.wait()

    scale = HD ** (-0.5) * math.log2(math.e)

    def attend(u, plane, row):
        kcol = pl.ds(pl.multiple_of(plane * HD, HD), HD)
        for i, t0, ks, kt in windows(row):
            key = kbuf[ks:ks + kt, kcol]
            val = vbuf[ks:ks + kt, kcol]
            for h in range(aw // HD):
                hc = pl.ds(pl.multiple_of(u * aw + h * HD, HD), HD)
                s = lax.dot_general(attn[t0:t0 + QT, hc], key, (((1,), (1,)), ((), ())),
                                    preferred_element_type=jnp.float32)
                s = s * scale + bias[i, :, :kt]
                m = jnp.max(s, axis=1, keepdims=True)
                p = jnp.exp2(s - m)
                tot = jnp.sum(p, axis=1, keepdims=True)
                o = jnp.dot(p.astype(jnp.bfloat16), val, preferred_element_type=jnp.float32)
                attn[t0:t0 + QT, hc] = (o / tot).astype(jnp.bfloat16)

    def attn_copy(u, rows):
        ref = attn.at[rows, pl.ds(pl.multiple_of(u * aw, aw), aw)]
        return pltpu.make_async_remote_copy(
            src_ref=ref, dst_ref=ref, send_sem=a_send.at[u], recv_sem=a_recv.at[u],
            device_id=partner, device_id_type=MESH)

    other_rows = pl.ds(pl.multiple_of((1 - r) * half, half), half)

    def attn_arrived(u):
        ref = attn.at[other_rows, pl.ds(pl.multiple_of(u * aw, aw), aw)]
        pltpu.make_async_copy(ref, ref, a_recv.at[u]).wait()

    hc = CH // 2

    def take(u, j, *ways):
        arrived(u, core, j)
        for way in ways:
            xfer(way, u, j).start()
        xfer(SIB, u, j).start()

    @pl.loop(0, POS)
    def _(g):
        u, plane = unit_at(g)

        @pl.when((r == 1) & (lax.rem(g, 2) == 0))
        def _():
            kv_remote(plane, 0).wait_recv()
            kv_remote(plane, 1).wait_recv()

        for row in range(2):
            @pl.when(r == row)
            def _():
                attend(u, plane, row)

        attn_copy(u, own_rows).start()

        j = g // 2

        @pl.when(is_end & (lax.rem(g, 2) == 1))
        def _():
            take(units[1], j, IN)
            arrived(units[2], core, j)

            @pl.when(j < hc)
            def _():
                xfer(ACROSS, units[2], j).start()

            xfer(SIB, units[2], j).start()

        @pl.when(is_mid & (lax.rem(g, 2) == 1))
        def _():
            take(units[4], j, OUT, ACROSS)
            take(units[2], j, IN)
            take(units[1], j)

    per = cw // NC

    def siblings(j, *positions):
        for pos in positions:
            arrived(units[pos], 1 - core, j)

    def feature(pos):
        return pl.ds(pl.multiple_of(units[pos] * aw, aw), aw)

    def add(i, *positions):
        w_cols = pl.ds(pl.multiple_of(lax.rem(i, per) * NC, NC), NC)
        for pos in positions:
            acc[:, part_cols(i)] += jnp.dot(attn[:, feature(pos)], wfull[units[pos], i // per, :, w_cols],
                                            preferred_element_type=jnp.float32)

    def square(start, count):
        @pl.loop(0, acc.shape[0] // 128)
        def _(b):
            rows = pl.ds(pl.multiple_of(b * 128, 128), 128)
            sqr = part[rows, :]
            for i in range(count // 128):
                a = acc[rows, pl.ds(pl.multiple_of(start + i * 128, 128), 128)]
                sqr += a * a
            part[rows, :] = sqr

    last = CH - 1
    sw = cw // NS
    T_OUT, T_ACROSS, T_SIB = 0, 1, 2
    t_units = (units[3], units[7])

    def piece(u, c, n):
        return wfull.at[u, last, pl.ds(pl.multiple_of(c * wrows, wrows), wrows),
                        pl.ds(pl.multiple_of(n * sw, sw), sw)]

    def t_xfer(kind, way, u, which, n):
        ref = piece(u, core, n)
        return pltpu.make_async_remote_copy(
            src_ref=ref, dst_ref=ref, send_sem=t_send.at[kind, n], recv_sem=t_recv.at[which, core, n],
            device_id=devices[way], device_id_type=MESH)

    def t_out(n):
        return t_xfer(T_OUT, OUT, units[1], 0, n)

    def t_across(n):
        return t_xfer(T_ACROSS, ACROSS, units[6], 1, n)

    def t_sib(which, n):
        return t_xfer(T_SIB + which, SIB, t_units[which], which, n)

    def t_arrived(which, c, n):
        ref = piece(t_units[which], c, n)
        pltpu.make_async_copy(ref, ref, t_recv.at[which, c, n]).wait()

    res_copy(0).start()
    res_copy(1).start()
    part[...] = jnp.zeros_like(part)

    @pl.loop(0, CH)
    def _(j):
        @pl.when(is_end)
        def _():
            take(units[4], j, ACROSS)
            late = (j >= hc) * 1
            take(units[3] + late * (units[5] - units[3]), j - late * hc)

        @pl.when(is_mid)
        def _():
            take(units[6], j, OUT, ACROSS)
            take(units[3], j)
            take(units[5], j)

        @pl.when(j == 0)
        def _():
            for pos in range(3):
                attn_arrived(units[pos])

        own_copy(j).wait()
        siblings(j, 0, 1, 2)

        @pl.loop(0, per)
        def _(e):
            i = j * per + e
            res_copy(i).wait()
            acc[:, part_cols(i)] = rbuf[lax.rem(i, 2)].astype(jnp.float32)

            @pl.when(i + 2 < CH * per)
            def _():
                res_copy(i + 2).start()

            add(i, 0, 1, 2)

    @pl.loop(0, hc)
    def _(j):
        @pl.when(is_end)
        def _():
            take(units[6], j, ACROSS)
            take(units[5], j + hc)

        @pl.when(is_mid & (j < hc - 1))
        def _():
            xfer(OUT, units[1], j + hc).start()

        @pl.when(is_mid & (j == hc - 1))
        def _():
            for n in range(NS):
                t_out(n).start()

        @pl.when(is_mid)
        def _():
            take(units[7], j)

        @pl.when(j == 0)
        def _():
            for pos in range(3, 6):
                attn_arrived(units[pos])

        siblings(j, 3, 4, 5)

        @pl.loop(0, per)
        def _(e):
            add(j * per + e, 3, 4, 5)

    @pl.loop(0, hc)
    def _(j):
        @pl.when(is_end)
        def _():
            arrived(units[6], core, j + hc)

            @pl.when(j < hc - 1)
            def _():
                xfer(ACROSS, units[6], j + hc).start()

            @pl.when(j == hc - 1)
            def _():
                for n in range(NS):
                    t_across(n).start()

            xfer(SIB, units[6], j + hc).start()
            take(units[7], j)

        @pl.when(is_mid)
        def _():
            take(units[7], j + hc)

        @pl.when(j == 0)
        def _():
            for pos in range(6, 8):
                attn_arrived(units[pos])

        siblings(j + hc, 4, 5, 6)
        siblings(j, 6, 7)

        @pl.loop(0, per)
        def _(e):
            i = j * per + e
            add(i + hc * per, 4, 5)
            add(i, 6, 7)
            square(i * NC, NC)

    def sent(way, pos, j):
        xfer(way, units[pos], j).wait_send()

    @pl.loop(0, hc * per)
    def _(i):
        add(hc * per + i, 6)

    @pl.loop(0, CH)
    def _(j):
        sent(IN, 0, j)
        sent(ACROSS, 0, j)
        sent(ACROSS, 4, j)
        for pos in (0, 1, 2, 4):
            sent(SIB, pos, j)

        @pl.when(is_end)
        def _():
            sent(IN, 1, j)

        @pl.when(is_mid)
        def _():
            sent(IN, 2, j)
            sent(OUT, 0, j)
            sent(OUT, 4, j)

    @pl.loop(hc, last)
    def _(j):
        @pl.when(is_end)
        def _():
            take(units[3], j)
            take(units[7], j)

        siblings(j, 3, 7)

        @pl.loop(0, per)
        def _(e):
            add(j * per + e, 3, 7)
            square((j * per + e) * NC, NC)

    @pl.when(is_mid)
    def _():
        siblings(last, 3, 7)

    def relay(n):
        for which in range(2):
            t_arrived(which, core, n)
            t_sib(which, n).start()

    @pl.when(is_end)
    def _():
        relay(0)

    @pl.loop(0, NS)
    def _(n):
        @pl.when(is_end & (n < NS - 1))
        def _():
            relay(n + 1)

        @pl.when(is_end)
        def _():
            for which in range(2):
                t_arrived(which, 1 - core, n)

        cols = pl.ds(pl.multiple_of(last * cw + n * sw, sw), sw)
        w_cols = pl.ds(pl.multiple_of(n * sw, sw), sw)
        for pos in (3, 7):
            acc[:, cols] += jnp.dot(attn[:, feature(pos)], wfull[units[pos], last, :, w_cols],
                                    preferred_element_type=jnp.float32)
        square(last * cw + n * sw, sw)

    sqbuf[0] = jnp.sum(part[...].T, axis=0, keepdims=True)
    x_sq = pltpu.make_async_remote_copy(
        src_ref=sqbuf.at[0], dst_ref=sqbuf.at[1], send_sem=x_send.at[0], recv_sem=x_recv.at[0],
        device_id=partner, device_id_type=MESH)
    x_sq.start()

    @pl.when(r == 0)
    def _():
        for plane in planes:
            kv_remote(plane, 0).wait_send()
            kv_remote(plane, 1).wait_send()

    @pl.loop(0, POS)
    def _(u):
        attn_copy(u, own_rows).wait_send()

    @pl.loop(0, last)
    def _(j):
        sent(ACROSS, 6, j)
        for pos in (3, 5, 6, 7):
            sent(SIB, pos, j)

    for pos in (5, 6):
        sent(SIB, pos, last)

    @pl.when(is_mid)
    def _():
        sent(ACROSS, 6, last)
        sent(SIB, 3, last)
        sent(SIB, 7, last)
        for j in range(CH):
            sent(OUT, 6, j)
        for j in range(hc, last):
            sent(OUT, 1, j)
        for n in range(NS):
            t_out(n).wait_send()

    @pl.when(is_end)
    def _():
        for j in range(hc):
            sent(ACROSS, 2, j)
        for n in range(NS):
            t_across(n).wait_send()
            t_sib(0, n).wait_send()
            t_sib(1, n).wait_send()

    x_sq.wait()
    sq_ref[...] = sqbuf[0] + sqbuf[1]


NR = 128


def norm_kernel(acc, sq_ref, gain_ref, sum_ref, out_ref, hbuf, nbuf, hsem, nsem):
    rows = acc.shape[0]

    def copies(i):
        block = pl.ds(pl.multiple_of(i * NR, NR), NR)
        return (pltpu.make_async_copy(hbuf.at[block, :], sum_ref.at[block, :], hsem.at[i]),
                pltpu.make_async_copy(nbuf.at[block, :], out_ref.at[block, :], nsem.at[i]))

    @pl.loop(0, rows // NR)
    def _(i):
        block = pl.ds(pl.multiple_of(i * NR, NR), NR)
        scaled = lax.rsqrt(sq_ref[:, block] / D + jnp.float32(1e-05))
        column = jnp.broadcast_to(scaled, (128, NR)).T[:, :1]
        for n in range(acc.shape[1] // 512):
            cols = slice(n * 512, (n + 1) * 512)
            hid = acc[block, cols]
            hbuf[block, cols] = hid.astype(jnp.bfloat16)
            nbuf[block, cols] = (hid * column * gain_ref[:, cols]).astype(jnp.bfloat16)
        for c in copies(i):
            c.start()

    @pl.loop(0, rows // NR)
    def _(i):
        for c in copies(i):
            c.wait()


def body_fused(query_proj, key_proj, value_proj, segment_ids, out_weight, residual, norm_gain):
    half, qw = query_proj.shape
    length = segment_ids.shape[1]
    wrows, width = out_weight.shape
    hbm = pl.BlockSpec(memory_space=pl.ANY)
    vmem = pl.BlockSpec(memory_space=pltpu.VMEM)
    dma = pltpu.SemaphoreType.DMA
    total, squares = pl.pallas_call(
        fused_kernel,
        out_shape=(
            pltpu.VMEM((length, width), jnp.float32),
            pltpu.VMEM((1, length), jnp.float32),
        ),
        in_specs=[hbm] * 6,
        out_specs=(vmem, vmem),
        scratch_shapes=[
            pltpu.VMEM((POS, CH, 2 * wrows, width // CH), jnp.bfloat16),
            pltpu.VMEM((2, length, HK * HD), jnp.bfloat16),
            pltpu.VMEM((half // QT, QT, KT), jnp.float32),
            pltpu.VMEM((length, qw), jnp.bfloat16),
            pltpu.VMEM((length, 128), jnp.float32),
            pltpu.VMEM((2, 1, length), jnp.float32),
            pltpu.VMEM((1, length), jnp.int32),
            dma((4, POS, CH)),
            dma((POS, 2, CH)),
            dma((4, NS)),
            dma((2, 2, NS)),
            dma((4,)),
            dma((CH,)),
            dma((2,)),
            dma((POS,)),
            dma((POS,)),
            dma((2, HK)),
            dma((2, HK)),
            dma((1,)),
            dma((1,)),
        ],
        compiler_params=pltpu.CompilerParams(
            collective_id=0, has_side_effects=True, vmem_limit_bytes=(47 * 1024 + 768) * 1024),
        name="fused",
    )(query_proj, key_proj, value_proj, segment_ids,
      out_weight, residual)
    total = pltpu.with_memory_space_constraint(total, pltpu.VMEM)
    squares = pltpu.with_memory_space_constraint(squares, pltpu.VMEM)
    return tuple(pl.pallas_call(
        norm_kernel,
        out_shape=(jax.ShapeDtypeStruct((length, width), jnp.bfloat16),) * 2,
        in_specs=[vmem, vmem, vmem],
        out_specs=(hbm, hbm),
        scratch_shapes=[
            pltpu.VMEM((length, width), jnp.bfloat16),
            pltpu.VMEM((length, width), jnp.bfloat16),
            dma((length // NR,)),
            dma((length // NR,)),
        ],
        compiler_params=pltpu.CompilerParams(vmem_limit_bytes=24 * 1024 * 1024),
        name="norm",
    )(total, squares, norm_gain.reshape(1, width)))


def solution(mesh):
    placed = (
        P(("col", "row"), None),
        P(("col", "row"), None),
        P(("col", "row"), None),
        P("col", None),
        P("col", "row"),
        P("col", "row"),
        P("row"),
    )
    known = mesh.shape["row"] == 2 and mesh.shape["col"] == 4 * NZ
    return jax.shard_map(
        body_fused if known else body_any,
        mesh=mesh,
        in_specs=placed,
        out_specs=(P("col", "row"), P("col", "row")),
        check_vma=False,
    )
```

```python
import functools
import math

import jax
import jax.numpy as jnp
from jax import lax
from jax.experimental import pallas as pl
from jax.experimental.pallas import tpu as pltpu
from jax.sharding import PartitionSpec as P

D = 8192
HD = 128
HK = 4
MESH = pl.DeviceIdType.MESH


def attend_local(query_heads, key_heads, value_heads, segment_row):
    length = query_heads.shape[0]
    kv_local = key_heads.shape[1] // HD
    group = query_heads.shape[1] // HD // kv_local
    query_grid = query_heads.reshape(length, kv_local, group, HD).transpose(1, 2, 0, 3)
    key_grid = key_heads.reshape(length, kv_local, HD).transpose(1, 0, 2)
    value_grid = value_heads.reshape(length, kv_local, HD).transpose(1, 0, 2)
    places = jnp.arange(length)
    allowed = (segment_row[:, None] == segment_row[None, :]) & (places[None, :] <= places[:, None])

    def one_group(operands):
        group_query, group_key, group_value = operands
        scores = jnp.einsum(
            "gqd,kd->gqk", group_query, group_key, preferred_element_type=jnp.float32
        ) * HD ** (-0.5)
        scores = jnp.where(allowed, scores, jnp.float32(-1e30))
        peak = jnp.max(scores, axis=-1, keepdims=True)
        weights = jnp.where(allowed, jnp.exp(scores - peak), jnp.float32(0.0))
        totals = jnp.sum(weights, axis=-1, keepdims=True)
        probs = weights.astype(jnp.bfloat16)
        mixture = (
            jnp.einsum("gqk,kd->gqd", probs, group_value, preferred_element_type=jnp.float32)
            / totals
        )
        return mixture.astype(jnp.bfloat16)

    heads_out = lax.map(one_group, (query_grid, key_grid, value_grid))
    return heads_out.transpose(2, 0, 1, 3).reshape(length, kv_local * group * HD)


def widen_heads(proj_rows, repeat):
    rows_local = proj_rows.shape[0]
    kv_count = proj_rows.shape[1] // HD
    if repeat == 1:
        return proj_rows
    spread = jnp.broadcast_to(
        proj_rows.reshape(rows_local, kv_count, 1, HD), (rows_local, kv_count, repeat, HD)
    )
    return spread.reshape(rows_local, kv_count * repeat * HD)


def body_any(query_proj, key_proj, value_proj, segment_ids, out_weight, residual, norm_gain):
    row_count = lax.axis_size("row")
    repeat = max(row_count // HK, 1)
    key_wide = widen_heads(key_proj, repeat)
    value_wide = widen_heads(value_proj, repeat)
    query_heads, key_heads, value_heads = (
        lax.all_to_all(query_proj, "row", split_axis=1, concat_axis=0, tiled=True),
        lax.all_to_all(key_wide, "row", split_axis=1, concat_axis=0, tiled=True),
        lax.all_to_all(value_wide, "row", split_axis=1, concat_axis=0, tiled=True),
    )
    attn = attend_local(query_heads, key_heads, value_heads, segment_ids[0])
    panel_rows = lax.all_gather(attn, "row", axis=1, tiled=True)
    projected = jnp.dot(
        panel_rows,
        lax.all_gather(out_weight, "col", axis=0, tiled=True),
        preferred_element_type=jnp.float32,
    )
    hidden_sum = residual.astype(jnp.float32) + projected
    squares = lax.psum(jnp.sum(hidden_sum * hidden_sum, axis=1), "row")
    scaled = lax.rsqrt(squares / D + jnp.float32(1e-05))
    normed = hidden_sum * scaled[:, None] * norm_gain[None, :]
    return (hidden_sum.astype(jnp.bfloat16), normed.astype(jnp.bfloat16))


NZ = 4
CH = 4
NC = 512
NS = 4
QT = 256
KT = 768
POS = 8
IN, OUT, ACROSS, SIB = range(4)


def fused_kernel(q_ref, k_ref, v_ref, seg_ref, w_ref, res_ref,
                 acc, sq_ref,
                 wfull, kvbuf, bias, attn, part, sqbuf, segbuf,
                 send, recv, t_send, t_recv, loc, wsem, rsem, a_send, a_recv, kv_send, kv_recv, x_send, x_recv):
    r = lax.axis_index("row")
    col = lax.axis_index("col")
    core = lax.rem(col, 2)
    y = lax.rem(col // 2, 2)
    z = col // 4
    half = q_ref.shape[0]
    wrows, width = w_ref.shape
    cw = width // CH
    aw = q_ref.shape[1] // POS

    end = 1 - (z * (3 - z)) // 2
    step = 1 - 2 * (z // 2)
    planes = (z, z + step * (2 * end - 1), z + step * (1 + end), z + step * (2 + end))
    is_end = end == 1
    is_mid = end == 0

    def cid(zz, yy, cc):
        return (zz * 2 + yy) * 2 + cc

    inner = (r, cid(z + step, y, core))
    outer = (r, cid(z - step, y, core))
    across = (r, cid(z, 1 - y, core))
    sibling = (r, cid(z, y, 1 - core))
    partner = (1 - r, col)
    devices = (inner, outer, across, sibling)

    def unit(pos):
        return planes[pos // 2] * 2 + (y if pos % 2 == 0 else 1 - y)

    units = [unit(pos) for pos in range(POS)]

    def unit_at(g):
        h = g // 2
        plane = planes[0] + (h == 1) * (planes[1] - planes[0])
        plane = plane + (h == 2) * (planes[2] - planes[0])
        plane = plane + (h == 3) * (planes[3] - planes[0])
        odd = lax.rem(g, 2)
        return plane * 2 + y + odd * (1 - 2 * y), plane

    barrier = pltpu.get_barrier_semaphore()

    def greet(dev):
        pl.semaphore_signal(barrier, inc=1, device_id=dev, device_id_type=MESH)

    greet(inner)
    greet(across)
    greet(sibling)
    greet(partner)

    @pl.when(is_mid)
    def _():
        greet(outer)

    kbuf, vbuf, rbuf = kvbuf.at[0], kvbuf.at[1], kvbuf

    own_rows = pl.ds(pl.multiple_of(r * half, half), half)
    k_local = pltpu.make_async_copy(k_ref, kbuf.at[own_rows, :], loc.at[0])
    v_local = pltpu.make_async_copy(v_ref, vbuf.at[own_rows, :], loc.at[1])
    q_local = pltpu.make_async_copy(q_ref, attn.at[own_rows, :], loc.at[2])
    seg_local = pltpu.make_async_copy(seg_ref, segbuf, loc.at[3])
    seg_local.start()
    q_local.start()
    k_local.start()
    v_local.start()

    @pl.when(is_end)
    def _():
        pl.semaphore_wait(barrier, 4)

    @pl.when(is_mid)
    def _():
        pl.semaphore_wait(barrier, 5)

    def cols_of(j):
        return pl.ds(pl.multiple_of(j * cw, cw), cw)

    def chunk(u, c, j):
        return wfull.at[u, j, pl.ds(pl.multiple_of(c * wrows, wrows), wrows), :]

    def own_copy(j):
        return pltpu.make_async_copy(w_ref.at[:, cols_of(j)], chunk(units[0], core, j), wsem.at[j])

    def xfer(way, u, j, own=False):
        dst = chunk(u, core, j)
        return pltpu.make_async_remote_copy(
            src_ref=w_ref.at[:, cols_of(j)] if own else dst, dst_ref=dst,
            send_sem=send.at[way, u, j], recv_sem=recv.at[u, core, j],
            device_id=devices[way], device_id_type=MESH)

    def arrived(u, c, j):
        ref = chunk(u, c, j)
        pltpu.make_async_copy(ref, ref, recv.at[u, c, j]).wait()

    def kv_remote(h, i):
        cols = pl.ds(pl.multiple_of(h * HD, HD), HD)
        src, dst = ((k_ref, kbuf), (v_ref, vbuf))[i]
        return pltpu.make_async_remote_copy(
            src_ref=src.at[:, cols], dst_ref=dst.at[pl.ds(0, half), cols],
            send_sem=kv_send.at[i, h], recv_sem=kv_recv.at[i, h],
            device_id=partner, device_id_type=MESH)

    @pl.loop(0, CH)
    def _(j):
        xfer(IN, units[0], j, True).start()

        @pl.when(is_mid)
        def _():
            xfer(OUT, units[0], j, True).start()

        xfer(ACROSS, units[0], j, True).start()

    @pl.when(r == 0)
    def _():
        for plane in planes:
            kv_remote(plane, 0).start()
            kv_remote(plane, 1).start()

    @pl.loop(0, CH)
    def _(j):
        xfer(SIB, units[0], j, True).start()
        own_copy(j).start()

    def part_cols(i):
        return pl.ds(pl.multiple_of(i * NC, NC), NC)

    def res_copy(i):
        slot = lax.rem(i, 2)
        return pltpu.make_async_copy(res_ref.at[:, part_cols(i)], rbuf.at[slot], rsem.at[slot])

    def mask(i, t0, ks, kt):
        qrow = segbuf[:, t0:t0 + QT].astype(jnp.float32)
        qs = jnp.broadcast_to(qrow, (128, QT)).T[:, :1]
        ksg = segbuf[:, ks:ks + kt].astype(jnp.float32)
        qp = t0 + lax.broadcasted_iota(jnp.int32, (QT, kt), 0)
        kp = ks + lax.broadcasted_iota(jnp.int32, (QT, kt), 1)
        keep = (qs == ksg) & (kp <= qp)
        bias[i, :, :kt] = jnp.where(keep, jnp.float32(0.0), jnp.float32(-1e30))

    def windows(row):
        out = []
        for i in range(half // QT):
            t0 = row * half + i * QT
            ks = max(t0 + QT - KT, 0)
            out.append((i, t0, ks, t0 + QT - ks))
        return out

    seg_local.wait()

    for row in range(2):
        @pl.when(r == row)
        def _():
            for w in windows(row):
                mask(*w)

    q_local.wait()
    k_local.wait()
    v_local.wait()

    scale = HD ** (-0.5) * math.log2(math.e)

    def attend(u, plane, row):
        kcol = pl.ds(pl.multiple_of(plane * HD, HD), HD)
        for i, t0, ks, kt in windows(row):
            key = kbuf[ks:ks + kt, kcol]
            val = vbuf[ks:ks + kt, kcol]
            for h in range(aw // HD):
                hc = pl.ds(pl.multiple_of(u * aw + h * HD, HD), HD)
                s = lax.dot_general(attn[t0:t0 + QT, hc], key, (((1,), (1,)), ((), ())),
                                    preferred_element_type=jnp.float32)
                s = s * scale + bias[i, :, :kt]
                m = jnp.max(s, axis=1, keepdims=True)
                p = jnp.exp2(s - m)
                tot = jnp.sum(p, axis=1, keepdims=True)
                o = jnp.dot(p.astype(jnp.bfloat16), val, preferred_element_type=jnp.float32)
                attn[t0:t0 + QT, hc] = (o / tot).astype(jnp.bfloat16)

    def attn_copy(u, rows):
        ref = attn.at[rows, pl.ds(pl.multiple_of(u * aw, aw), aw)]
        return pltpu.make_async_remote_copy(
            src_ref=ref, dst_ref=ref, send_sem=a_send.at[u], recv_sem=a_recv.at[u],
            device_id=partner, device_id_type=MESH)

    other_rows = pl.ds(pl.multiple_of((1 - r) * half, half), half)

    def attn_arrived(u):
        ref = attn.at[other_rows, pl.ds(pl.multiple_of(u * aw, aw), aw)]
        pltpu.make_async_copy(ref, ref, a_recv.at[u]).wait()

    hc = CH // 2

    def take(u, j, *ways):
        arrived(u, core, j)
        for way in ways:
            xfer(way, u, j).start()
        xfer(SIB, u, j).start()

    @pl.loop(0, POS)
    def _(g):
        u, plane = unit_at(g)

        @pl.when((r == 1) & (lax.rem(g, 2) == 0))
        def _():
            kv_remote(plane, 0).wait_recv()
            kv_remote(plane, 1).wait_recv()

        for row in range(2):
            @pl.when(r == row)
            def _():
                attend(u, plane, row)

        attn_copy(u, own_rows).start()

        j = g // 2

        @pl.when(is_end & (lax.rem(g, 2) == 1))
        def _():
            take(units[1], j, IN)
            arrived(units[2], core, j)

            @pl.when(j < hc)
            def _():
                xfer(ACROSS, units[2], j).start()

            xfer(SIB, units[2], j).start()

        @pl.when(is_mid & (lax.rem(g, 2) == 1))
        def _():
            take(units[4], j, OUT, ACROSS)
            take(units[2], j, IN)
            take(units[1], j)

    per = cw // NC

    def siblings(j, *positions):
        for pos in positions:
            arrived(units[pos], 1 - core, j)

    def feature(pos):
        return pl.ds(pl.multiple_of(units[pos] * aw, aw), aw)

    def add(i, *positions):
        w_cols = pl.ds(pl.multiple_of(lax.rem(i, per) * NC, NC), NC)
        for pos in positions:
            acc[:, part_cols(i)] += jnp.dot(attn[:, feature(pos)], wfull[units[pos], i // per, :, w_cols],
                                            preferred_element_type=jnp.float32)

    def square(start, count):
        @pl.loop(0, acc.shape[0] // 128)
        def _(b):
            rows = pl.ds(pl.multiple_of(b * 128, 128), 128)
            sqr = part[rows, :]
            for i in range(count // 128):
                a = acc[rows, pl.ds(pl.multiple_of(start + i * 128, 128), 128)]
                sqr += a * a
            part[rows, :] = sqr

    last = CH - 1
    sw = cw // NS
    T_OUT, T_ACROSS, T_SIB = 0, 1, 2
    t_units = (units[3], units[7])

    def piece(u, c, n):
        return wfull.at[u, last, pl.ds(pl.multiple_of(c * wrows, wrows), wrows),
                        pl.ds(pl.multiple_of(n * sw, sw), sw)]

    def t_xfer(kind, way, u, which, n):
        ref = piece(u, core, n)
        return pltpu.make_async_remote_copy(
            src_ref=ref, dst_ref=ref, send_sem=t_send.at[kind, n], recv_sem=t_recv.at[which, core, n],
            device_id=devices[way], device_id_type=MESH)

    def t_out(n):
        return t_xfer(T_OUT, OUT, units[1], 0, n)

    def t_across(n):
        return t_xfer(T_ACROSS, ACROSS, units[6], 1, n)

    def t_sib(which, n):
        return t_xfer(T_SIB + which, SIB, t_units[which], which, n)

    def t_arrived(which, c, n):
        ref = piece(t_units[which], c, n)
        pltpu.make_async_copy(ref, ref, t_recv.at[which, c, n]).wait()

    res_copy(0).start()
    res_copy(1).start()
    part[...] = jnp.zeros_like(part)

    @pl.loop(0, CH)
    def _(j):
        @pl.when(is_end)
        def _():
            take(units[4], j, ACROSS)
            late = (j >= hc) * 1
            take(units[3] + late * (units[5] - units[3]), j - late * hc)

        @pl.when(is_mid)
        def _():
            take(units[6], j, OUT, ACROSS)
            take(units[3], j)
            take(units[5], j)

        @pl.when(j == 0)
        def _():
            for pos in range(3):
                attn_arrived(units[pos])

        own_copy(j).wait()
        siblings(j, 0, 1, 2)

        @pl.loop(0, per)
        def _(e):
            i = j * per + e
            res_copy(i).wait()
            acc[:, part_cols(i)] = rbuf[lax.rem(i, 2)].astype(jnp.float32)

            @pl.when(i + 2 < CH * per)
            def _():
                res_copy(i + 2).start()

            add(i, 0, 1, 2)

    @pl.loop(0, hc)
    def _(j):
        @pl.when(is_end)
        def _():
            take(units[6], j, ACROSS)
            take(units[5], j + hc)

        @pl.when(is_mid & (j < hc - 1))
        def _():
            xfer(OUT, units[1], j + hc).start()

        @pl.when(is_mid & (j == hc - 1))
        def _():
            for n in range(NS):
                t_out(n).start()

        @pl.when(is_mid)
        def _():
            take(units[7], j)

        @pl.when(j == 0)
        def _():
            for pos in range(3, 6):
                attn_arrived(units[pos])

        siblings(j, 3, 4, 5)

        @pl.loop(0, per)
        def _(e):
            add(j * per + e, 3, 4, 5)

    @pl.loop(0, hc)
    def _(j):
        @pl.when(is_end)
        def _():
            arrived(units[6], core, j + hc)

            @pl.when(j < hc - 1)
            def _():
                xfer(ACROSS, units[6], j + hc).start()

            @pl.when(j == hc - 1)
            def _():
                for n in range(NS):
                    t_across(n).start()

            xfer(SIB, units[6], j + hc).start()
            take(units[7], j)

        @pl.when(is_mid)
        def _():
            take(units[7], j + hc)

        @pl.when(j == 0)
        def _():
            for pos in range(6, 8):
                attn_arrived(units[pos])

        siblings(j + hc, 4, 5, 6)
        siblings(j, 6, 7)

        @pl.loop(0, per)
        def _(e):
            i = j * per + e
            add(i + hc * per, 4, 5)
            add(i, 6, 7)
            square(i * NC, NC)

    def sent(way, pos, j):
        xfer(way, units[pos], j).wait_send()

    @pl.loop(0, hc * per)
    def _(i):
        add(hc * per + i, 6)

    @pl.loop(0, CH)
    def _(j):
        sent(IN, 0, j)
        sent(ACROSS, 0, j)
        sent(ACROSS, 4, j)
        for pos in (0, 1, 2, 4):
            sent(SIB, pos, j)

        @pl.when(is_end)
        def _():
            sent(IN, 1, j)

        @pl.when(is_mid)
        def _():
            sent(IN, 2, j)
            sent(OUT, 0, j)
            sent(OUT, 4, j)

    @pl.loop(hc, last)
    def _(j):
        @pl.when(is_end)
        def _():
            take(units[3], j)
            take(units[7], j)

        siblings(j, 3, 7)

        @pl.loop(0, per)
        def _(e):
            add(j * per + e, 3, 7)
            square((j * per + e) * NC, NC)

    @pl.when(r == 0)
    def _():
        for plane in planes:
            kv_remote(plane, 0).wait_send()
            kv_remote(plane, 1).wait_send()

    @pl.loop(0, POS)
    def _(u):
        attn_copy(u, own_rows).wait_send()

    @pl.loop(0, last)
    def _(j):
        sent(ACROSS, 6, j)
        for pos in (3, 5, 6, 7):
            sent(SIB, pos, j)

    @pl.when(is_mid)
    def _():
        siblings(last, 3, 7)

    def relay(n):
        for which in range(2):
            t_arrived(which, core, n)
            t_sib(which, n).start()

    @pl.when(is_end)
    def _():
        relay(0)

    @pl.loop(0, NS)
    def _(n):
        @pl.when(is_end & (n < NS - 1))
        def _():
            relay(n + 1)

        @pl.when(is_end)
        def _():
            for which in range(2):
                t_arrived(which, 1 - core, n)

        cols = pl.ds(pl.multiple_of(last * cw + n * sw, sw), sw)
        w_cols = pl.ds(pl.multiple_of(n * sw, sw), sw)
        for b in range(acc.shape[0] // 256):
            rows = pl.ds(b * 256, 256)
            val = acc[rows, cols]
            for pos in (3, 7):
                val += jnp.dot(attn[rows, feature(pos)], wfull[units[pos], last, :, w_cols],
                               preferred_element_type=jnp.float32)
            acc[rows, cols] = val
            part[rows, :] += sum(val[:, k * 128:(k + 1) * 128] ** 2 for k in range(sw // 128))

    sqbuf[0] = jnp.sum(part[...].T, axis=0, keepdims=True)
    x_sq = pltpu.make_async_remote_copy(
        src_ref=sqbuf.at[0], dst_ref=sqbuf.at[1], send_sem=x_send.at[0], recv_sem=x_recv.at[0],
        device_id=partner, device_id_type=MESH)
    x_sq.start()

    for pos in (5, 6):
        sent(SIB, pos, last)

    @pl.when(is_mid)
    def _():
        sent(ACROSS, 6, last)
        sent(SIB, 3, last)
        sent(SIB, 7, last)
        @pl.loop(0, CH)
        def _(j):
            sent(OUT, 6, j)

        for j in range(hc, last):
            sent(OUT, 1, j)
        for n in range(NS):
            t_out(n).wait_send()

    @pl.when(is_end)
    def _():
        for j in range(hc):
            sent(ACROSS, 2, j)
        for n in range(NS):
            t_across(n).wait_send()
            t_sib(0, n).wait_send()
            t_sib(1, n).wait_send()

    x_sq.wait()
    sq_ref[...] = sqbuf[0] + sqbuf[1]


NR = 128


def norm_kernel(acc, sq_ref, gain_ref, sum_ref, out_ref, hbuf, nbuf, hsem, nsem):
    rows = acc.shape[0]

    def copies(i):
        block = pl.ds(pl.multiple_of(i * NR, NR), NR)
        return (pltpu.make_async_copy(hbuf.at[block, :], sum_ref.at[block, :], hsem.at[i]),
                pltpu.make_async_copy(nbuf.at[block, :], out_ref.at[block, :], nsem.at[i]))

    @pl.loop(0, rows // NR)
    def _(i):
        block = pl.ds(pl.multiple_of(i * NR, NR), NR)
        scaled = lax.rsqrt(sq_ref[:, block] / D + jnp.float32(1e-05))
        column = jnp.broadcast_to(scaled, (128, NR)).T[:, :1]
        hid_copy, norm_copy = copies(i)
        for n in range(acc.shape[1] // 512):
            cols = slice(n * 512, (n + 1) * 512)
            hbuf[block, cols] = acc[block, cols].astype(jnp.bfloat16)
        hid_copy.start()
        for n in range(acc.shape[1] // 512):
            cols = slice(n * 512, (n + 1) * 512)
            nbuf[block, cols] = (acc[block, cols] * column * gain_ref[:, cols]).astype(jnp.bfloat16)
        norm_copy.start()

    @pl.loop(0, rows // NR)
    def _(i):
        for c in copies(i):
            c.wait()


def body_fused(query_proj, key_proj, value_proj, segment_ids, out_weight, residual, norm_gain):
    half, qw = query_proj.shape
    length = segment_ids.shape[1]
    wrows, width = out_weight.shape
    hbm = pl.BlockSpec(memory_space=pl.ANY)
    vmem = pl.BlockSpec(memory_space=pltpu.VMEM)
    dma = pltpu.SemaphoreType.DMA
    total, squares = pl.pallas_call(
        fused_kernel,
        out_shape=(
            pltpu.VMEM((length, width), jnp.float32),
            pltpu.VMEM((1, length), jnp.float32),
        ),
        in_specs=[hbm] * 6,
        out_specs=(vmem, vmem),
        scratch_shapes=[
            pltpu.VMEM((POS, CH, 2 * wrows, width // CH), jnp.bfloat16),
            pltpu.VMEM((2, length, HK * HD), jnp.bfloat16),
            pltpu.VMEM((half // QT, QT, KT), jnp.float32),
            pltpu.VMEM((length, qw), jnp.bfloat16),
            pltpu.VMEM((length, 128), jnp.float32),
            pltpu.VMEM((2, 1, length), jnp.float32),
            pltpu.VMEM((1, length), jnp.int32),
            dma((4, POS, CH)),
            dma((POS, 2, CH)),
            dma((4, NS)),
            dma((2, 2, NS)),
            dma((4,)),
            dma((CH,)),
            dma((2,)),
            dma((POS,)),
            dma((POS,)),
            dma((2, HK)),
            dma((2, HK)),
            dma((1,)),
            dma((1,)),
        ],
        compiler_params=pltpu.CompilerParams(
            collective_id=0, has_side_effects=True, vmem_limit_bytes=(47 * 1024 + 768) * 1024),
        name="fused",
    )(query_proj, key_proj, value_proj, segment_ids,
      out_weight, residual)
    total = pltpu.with_memory_space_constraint(total, pltpu.VMEM)
    squares = pltpu.with_memory_space_constraint(squares, pltpu.VMEM)
    return tuple(pl.pallas_call(
        norm_kernel,
        out_shape=(jax.ShapeDtypeStruct((length, width), jnp.bfloat16),) * 2,
        in_specs=[vmem, vmem, vmem],
        out_specs=(hbm, hbm),
        scratch_shapes=[
            pltpu.VMEM((length, width), jnp.bfloat16),
            pltpu.VMEM((length, width), jnp.bfloat16),
            dma((length // NR,)),
            dma((length // NR,)),
        ],
        compiler_params=pltpu.CompilerParams(vmem_limit_bytes=24 * 1024 * 1024),
        name="norm",
    )(total, squares, norm_gain.reshape(1, width)))


def solution(mesh):
    placed = (
        P(("col", "row"), None),
        P(("col", "row"), None),
        P(("col", "row"), None),
        P("col", None),
        P("col", "row"),
        P("col", "row"),
        P("row"),
    )
    known = mesh.shape["row"] == 2 and mesh.shape["col"] == 4 * NZ
    return jax.shard_map(
        body_fused if known else body_any,
        mesh=mesh,
        in_specs=placed,
        out_specs=(P("col", "row"), P("col", "row")),
        check_vma=False,
    )
```

```python
import functools
import math

import jax
import jax.numpy as jnp
from jax import lax
from jax.experimental import pallas as pl
from jax.experimental.pallas import tpu as pltpu
from jax.sharding import PartitionSpec as P

D = 8192
HD = 128
HK = 4
MESH = pl.DeviceIdType.MESH


def attend_local(query_heads, key_heads, value_heads, segment_row):
    length = query_heads.shape[0]
    kv_local = key_heads.shape[1] // HD
    group = query_heads.shape[1] // HD // kv_local
    query_grid = query_heads.reshape(length, kv_local, group, HD).transpose(1, 2, 0, 3)
    key_grid = key_heads.reshape(length, kv_local, HD).transpose(1, 0, 2)
    value_grid = value_heads.reshape(length, kv_local, HD).transpose(1, 0, 2)
    places = jnp.arange(length)
    allowed = (segment_row[:, None] == segment_row[None, :]) & (places[None, :] <= places[:, None])

    def one_group(operands):
        group_query, group_key, group_value = operands
        scores = jnp.einsum(
            "gqd,kd->gqk", group_query, group_key, preferred_element_type=jnp.float32
        ) * HD ** (-0.5)
        scores = jnp.where(allowed, scores, jnp.float32(-1e30))
        peak = jnp.max(scores, axis=-1, keepdims=True)
        weights = jnp.where(allowed, jnp.exp(scores - peak), jnp.float32(0.0))
        totals = jnp.sum(weights, axis=-1, keepdims=True)
        probs = weights.astype(jnp.bfloat16)
        mixture = (
            jnp.einsum("gqk,kd->gqd", probs, group_value, preferred_element_type=jnp.float32)
            / totals
        )
        return mixture.astype(jnp.bfloat16)

    heads_out = lax.map(one_group, (query_grid, key_grid, value_grid))
    return heads_out.transpose(2, 0, 1, 3).reshape(length, kv_local * group * HD)


def widen_heads(proj_rows, repeat):
    rows_local = proj_rows.shape[0]
    kv_count = proj_rows.shape[1] // HD
    if repeat == 1:
        return proj_rows
    spread = jnp.broadcast_to(
        proj_rows.reshape(rows_local, kv_count, 1, HD), (rows_local, kv_count, repeat, HD)
    )
    return spread.reshape(rows_local, kv_count * repeat * HD)


def body_any(query_proj, key_proj, value_proj, segment_ids, out_weight, residual, norm_gain):
    row_count = lax.axis_size("row")
    repeat = max(row_count // HK, 1)
    key_wide = widen_heads(key_proj, repeat)
    value_wide = widen_heads(value_proj, repeat)
    query_heads, key_heads, value_heads = (
        lax.all_to_all(query_proj, "row", split_axis=1, concat_axis=0, tiled=True),
        lax.all_to_all(key_wide, "row", split_axis=1, concat_axis=0, tiled=True),
        lax.all_to_all(value_wide, "row", split_axis=1, concat_axis=0, tiled=True),
    )
    attn = attend_local(query_heads, key_heads, value_heads, segment_ids[0])
    panel_rows = lax.all_gather(attn, "row", axis=1, tiled=True)
    projected = jnp.dot(
        panel_rows,
        lax.all_gather(out_weight, "col", axis=0, tiled=True),
        preferred_element_type=jnp.float32,
    )
    hidden_sum = residual.astype(jnp.float32) + projected
    squares = lax.psum(jnp.sum(hidden_sum * hidden_sum, axis=1), "row")
    scaled = lax.rsqrt(squares / D + jnp.float32(1e-05))
    normed = hidden_sum * scaled[:, None] * norm_gain[None, :]
    return (hidden_sum.astype(jnp.bfloat16), normed.astype(jnp.bfloat16))


NZ = 4
CH = 4
NC = 512
NS = 4
QT = 256
KT = 768
POS = 8
IN, OUT, ACROSS, SIB = range(4)


def fused_kernel(q_ref, k_ref, v_ref, seg_ref, w_ref, res_ref,
                 acc, sq_ref,
                 wfull, kvbuf, bias, attn, part, sqbuf, segbuf,
                 send, recv, t_send, t_recv, loc, wsem, rsem, a_send, a_recv, kv_send, kv_recv, x_send, x_recv):
    r = lax.axis_index("row")
    col = lax.axis_index("col")
    core = lax.rem(col, 2)
    y = lax.rem(col // 2, 2)
    z = col // 4
    half = q_ref.shape[0]
    wrows, width = w_ref.shape
    cw = width // CH
    aw = q_ref.shape[1] // POS

    end = 1 - (z * (3 - z)) // 2
    step = 1 - 2 * (z // 2)
    planes = (z, z + step * (2 * end - 1), z + step * (1 + end), z + step * (2 + end))
    is_end = end == 1
    is_mid = end == 0

    def cid(zz, yy, cc):
        return (zz * 2 + yy) * 2 + cc

    inner = (r, cid(z + step, y, core))
    outer = (r, cid(z - step, y, core))
    across = (r, cid(z, 1 - y, core))
    sibling = (r, cid(z, y, 1 - core))
    partner = (1 - r, col)
    devices = (inner, outer, across, sibling)

    def unit(pos):
        return planes[pos // 2] * 2 + (y if pos % 2 == 0 else 1 - y)

    units = [unit(pos) for pos in range(POS)]

    def unit_at(g):
        h = g // 2
        plane = planes[0] + (h == 1) * (planes[1] - planes[0])
        plane = plane + (h == 2) * (planes[2] - planes[0])
        plane = plane + (h == 3) * (planes[3] - planes[0])
        odd = lax.rem(g, 2)
        return plane * 2 + y + odd * (1 - 2 * y), plane

    barrier = pltpu.get_barrier_semaphore()

    def greet(dev):
        pl.semaphore_signal(barrier, inc=1, device_id=dev, device_id_type=MESH)

    greet(inner)
    greet(across)
    greet(sibling)
    greet(partner)

    @pl.when(is_mid)
    def _():
        greet(outer)

    kbuf, vbuf, rbuf = kvbuf.at[0], kvbuf.at[1], kvbuf

    own_rows = pl.ds(pl.multiple_of(r * half, half), half)
    k_local = pltpu.make_async_copy(k_ref, kbuf.at[own_rows, :], loc.at[0])
    v_local = pltpu.make_async_copy(v_ref, vbuf.at[own_rows, :], loc.at[1])
    q_local = pltpu.make_async_copy(q_ref, attn.at[own_rows, :], loc.at[2])
    seg_local = pltpu.make_async_copy(seg_ref, segbuf, loc.at[3])

    @pl.when(is_end)
    def _():
        pl.semaphore_wait(barrier, 4)

    @pl.when(is_mid)
    def _():
        pl.semaphore_wait(barrier, 5)

    def cols_of(j):
        return pl.ds(pl.multiple_of(j * cw, cw), cw)

    def chunk(u, c, j):
        return wfull.at[u, j, pl.ds(pl.multiple_of(c * wrows, wrows), wrows), :]

    def own_copy(j):
        return pltpu.make_async_copy(w_ref.at[:, cols_of(j)], chunk(units[0], core, j), wsem.at[j])

    def xfer(way, u, j, own=False):
        dst = chunk(u, core, j)
        return pltpu.make_async_remote_copy(
            src_ref=w_ref.at[:, cols_of(j)] if own else dst, dst_ref=dst,
            send_sem=send.at[way, u, j], recv_sem=recv.at[u, core, j],
            device_id=devices[way], device_id_type=MESH)

    def arrived(u, c, j):
        ref = chunk(u, c, j)
        pltpu.make_async_copy(ref, ref, recv.at[u, c, j]).wait()

    def kv_remote(h, i):
        cols = pl.ds(pl.multiple_of(h * HD, HD), HD)
        src, dst = ((k_ref, kbuf), (v_ref, vbuf))[i]
        return pltpu.make_async_remote_copy(
            src_ref=src.at[:, cols], dst_ref=dst.at[pl.ds(0, half), cols],
            send_sem=kv_send.at[i, h], recv_sem=kv_recv.at[i, h],
            device_id=partner, device_id_type=MESH)

    @pl.loop(0, CH)
    def _(j):
        @pl.when(is_mid)
        def _():
            xfer(OUT, units[0], j, True).start()

        xfer(ACROSS, units[0], j, True).start()
        xfer(IN, units[0], j, True).start()

    seg_local.start()
    q_local.start()
    k_local.start()
    v_local.start()

    @pl.when(r == 0)
    def _():
        for plane in planes:
            kv_remote(plane, 0).start()
            kv_remote(plane, 1).start()

    @pl.loop(0, CH)
    def _(j):
        xfer(SIB, units[0], j, True).start()
        own_copy(j).start()

    def part_cols(i):
        return pl.ds(pl.multiple_of(i * NC, NC), NC)

    def res_copy(i):
        slot = lax.rem(i, 2)
        return pltpu.make_async_copy(res_ref.at[:, part_cols(i)], rbuf.at[slot], rsem.at[slot])

    def mask(i, t0, ks, kt):
        qrow = segbuf[:, t0:t0 + QT].astype(jnp.float32)
        qs = jnp.broadcast_to(qrow, (128, QT)).T[:, :1]
        ksg = segbuf[:, ks:ks + kt].astype(jnp.float32)
        qp = t0 + lax.broadcasted_iota(jnp.int32, (QT, kt), 0)
        kp = ks + lax.broadcasted_iota(jnp.int32, (QT, kt), 1)
        keep = (qs == ksg) & (kp <= qp)
        bias[i, :, :kt] = jnp.where(keep, jnp.float32(0.0), jnp.float32(-1e30))

    def windows(row):
        out = []
        for i in range(half // QT):
            t0 = row * half + i * QT
            ks = max(t0 + QT - KT, 0)
            out.append((i, t0, ks, t0 + QT - ks))
        return out

    seg_local.wait()

    for row in range(2):
        @pl.when(r == row)
        def _():
            for w in windows(row):
                mask(*w)

    q_local.wait()
    k_local.wait()
    v_local.wait()

    scale = HD ** (-0.5) * math.log2(math.e)

    def attend(u, plane, row):
        kcol = pl.ds(pl.multiple_of(plane * HD, HD), HD)
        for i, t0, ks, kt in windows(row):
            key = kbuf[ks:ks + kt, kcol]
            val = vbuf[ks:ks + kt, kcol]
            for h in range(aw // HD):
                hc = pl.ds(pl.multiple_of(u * aw + h * HD, HD), HD)
                s = lax.dot_general(attn[t0:t0 + QT, hc], key, (((1,), (1,)), ((), ())),
                                    preferred_element_type=jnp.float32)
                s = s * scale + bias[i, :, :kt]
                m = jnp.max(s, axis=1, keepdims=True)
                p = jnp.exp2(s - m)
                tot = jnp.sum(p, axis=1, keepdims=True)
                o = jnp.dot(p.astype(jnp.bfloat16), val, preferred_element_type=jnp.float32)
                attn[t0:t0 + QT, hc] = (o / tot).astype(jnp.bfloat16)

    def attn_copy(u, rows):
        ref = attn.at[rows, pl.ds(pl.multiple_of(u * aw, aw), aw)]
        return pltpu.make_async_remote_copy(
            src_ref=ref, dst_ref=ref, send_sem=a_send.at[u], recv_sem=a_recv.at[u],
            device_id=partner, device_id_type=MESH)

    other_rows = pl.ds(pl.multiple_of((1 - r) * half, half), half)

    def attn_arrived(u):
        ref = attn.at[other_rows, pl.ds(pl.multiple_of(u * aw, aw), aw)]
        pltpu.make_async_copy(ref, ref, a_recv.at[u]).wait()

    hc = CH // 2

    def take(u, j, *ways):
        arrived(u, core, j)
        for way in ways:
            xfer(way, u, j).start()
        xfer(SIB, u, j).start()

    @pl.loop(0, POS)
    def _(g):
        u, plane = unit_at(g)

        @pl.when((r == 1) & (lax.rem(g, 2) == 0))
        def _():
            kv_remote(plane, 0).wait_recv()
            kv_remote(plane, 1).wait_recv()

        for row in range(2):
            @pl.when(r == row)
            def _():
                attend(u, plane, row)

        attn_copy(u, own_rows).start()

        j = g // 2

        @pl.when(is_end & (lax.rem(g, 2) == 1))
        def _():
            take(units[1], j, IN)
            arrived(units[2], core, j)

            @pl.when(j < hc)
            def _():
                xfer(ACROSS, units[2], j).start()

            xfer(SIB, units[2], j).start()

        @pl.when(is_mid & (lax.rem(g, 2) == 1))
        def _():
            take(units[4], j, OUT, ACROSS)
            take(units[2], j, IN)
            take(units[1], j)

    per = cw // NC

    def siblings(j, *positions):
        for pos in positions:
            arrived(units[pos], 1 - core, j)

    def feature(pos):
        return pl.ds(pl.multiple_of(units[pos] * aw, aw), aw)

    def add(i, *positions):
        w_cols = pl.ds(pl.multiple_of(lax.rem(i, per) * NC, NC), NC)
        for pos in positions:
            acc[:, part_cols(i)] += jnp.dot(attn[:, feature(pos)], wfull[units[pos], i // per, :, w_cols],
                                            preferred_element_type=jnp.float32)

    def square(start, count):
        @pl.loop(0, acc.shape[0] // 128)
        def _(b):
            rows = pl.ds(pl.multiple_of(b * 128, 128), 128)
            sqr = part[rows, :]
            for i in range(count // 128):
                a = acc[rows, pl.ds(pl.multiple_of(start + i * 128, 128), 128)]
                sqr += a * a
            part[rows, :] = sqr

    last = CH - 1
    sw = cw // NS
    T_OUT, T_ACROSS, T_SIB = 0, 1, 2
    t_units = (units[3], units[7])

    def piece(u, c, n):
        return wfull.at[u, last, pl.ds(pl.multiple_of(c * wrows, wrows), wrows),
                        pl.ds(pl.multiple_of(n * sw, sw), sw)]

    def t_xfer(kind, way, u, which, n):
        ref = piece(u, core, n)
        return pltpu.make_async_remote_copy(
            src_ref=ref, dst_ref=ref, send_sem=t_send.at[kind, n], recv_sem=t_recv.at[which, core, n],
            device_id=devices[way], device_id_type=MESH)

    def t_out(n):
        return t_xfer(T_OUT, OUT, units[1], 0, n)

    def t_across(n):
        return t_xfer(T_ACROSS, ACROSS, units[6], 1, n)

    def t_sib(which, n):
        return t_xfer(T_SIB + which, SIB, t_units[which], which, n)

    def t_arrived(which, c, n):
        ref = piece(t_units[which], c, n)
        pltpu.make_async_copy(ref, ref, t_recv.at[which, c, n]).wait()

    res_copy(0).start()
    res_copy(1).start()
    part[...] = jnp.zeros_like(part)

    @pl.loop(0, CH)
    def _(j):
        @pl.when(is_end)
        def _():
            take(units[4], j, ACROSS)
            late = (j >= hc) * 1
            take(units[3] + late * (units[5] - units[3]), j - late * hc)

        @pl.when(is_mid)
        def _():
            take(units[6], j, OUT, ACROSS)
            take(units[3], j)
            take(units[5], j)

        @pl.when(j == 0)
        def _():
            for pos in range(3):
                attn_arrived(units[pos])

        own_copy(j).wait()
        siblings(j, 0, 1, 2)

        @pl.loop(0, per)
        def _(e):
            i = j * per + e
            res_copy(i).wait()
            acc[:, part_cols(i)] = rbuf[lax.rem(i, 2)].astype(jnp.float32)

            @pl.when(i + 2 < CH * per)
            def _():
                res_copy(i + 2).start()

            add(i, 0, 1, 2)

    @pl.loop(0, hc)
    def _(j):
        @pl.when(is_end)
        def _():
            take(units[6], j, ACROSS)
            take(units[5], j + hc)

        @pl.when(is_mid & (j < hc - 1))
        def _():
            xfer(OUT, units[1], j + hc).start()

        @pl.when(is_mid & (j == hc - 1))
        def _():
            for n in range(NS):
                t_out(n).start()

        @pl.when(is_mid)
        def _():
            take(units[7], j)

        @pl.when(j == 0)
        def _():
            for pos in range(3, 6):
                attn_arrived(units[pos])

        siblings(j, 3, 4, 5)

        @pl.loop(0, per)
        def _(e):
            add(j * per + e, 3, 4, 5)

    @pl.loop(0, hc)
    def _(j):
        @pl.when(is_end)
        def _():
            arrived(units[6], core, j + hc)

            @pl.when(j < hc - 1)
            def _():
                xfer(ACROSS, units[6], j + hc).start()

            @pl.when(j == hc - 1)
            def _():
                for n in range(NS):
                    t_across(n).start()

            xfer(SIB, units[6], j + hc).start()
            take(units[7], j)

        @pl.when(is_mid)
        def _():
            take(units[7], j + hc)

        @pl.when(j == 0)
        def _():
            for pos in range(6, 8):
                attn_arrived(units[pos])

        siblings(j + hc, 4, 5, 6)
        siblings(j, 6, 7)

        @pl.loop(0, per)
        def _(e):
            i = j * per + e
            add(i + hc * per, 4, 5)
            add(i, 6, 7)
            square(i * NC, NC)

    def sent(way, pos, j):
        xfer(way, units[pos], j).wait_send()

    @pl.loop(0, hc * per)
    def _(i):
        add(hc * per + i, 6)

    @pl.loop(0, CH)
    def _(j):
        sent(IN, 0, j)
        sent(ACROSS, 0, j)
        sent(ACROSS, 4, j)
        for pos in (0, 1, 2, 4):
            sent(SIB, pos, j)

        @pl.when(is_end)
        def _():
            sent(IN, 1, j)

        @pl.when(is_mid)
        def _():
            sent(IN, 2, j)
            sent(OUT, 0, j)
            sent(OUT, 4, j)

    @pl.loop(hc, last)
    def _(j):
        @pl.when(is_end)
        def _():
            take(units[3], j)
            take(units[7], j)

        siblings(j, 3, 7)

        @pl.loop(0, per)
        def _(e):
            add(j * per + e, 3, 7)
            square((j * per + e) * NC, NC)

    @pl.when(r == 0)
    def _():
        for plane in planes:
            kv_remote(plane, 0).wait_send()
            kv_remote(plane, 1).wait_send()

    @pl.loop(0, POS)
    def _(u):
        attn_copy(u, own_rows).wait_send()

    @pl.loop(0, last)
    def _(j):
        sent(ACROSS, 6, j)
        for pos in (3, 5, 6, 7):
            sent(SIB, pos, j)

    @pl.when(is_mid)
    def _():
        siblings(last, 3, 7)

    def relay(n):
        for which in range(2):
            t_arrived(which, core, n)
            t_sib(which, n).start()

    @pl.when(is_end)
    def _():
        relay(0)

    @pl.loop(0, NS)
    def _(n):
        @pl.when(is_end & (n < NS - 1))
        def _():
            relay(n + 1)

        @pl.when(is_end)
        def _():
            for which in range(2):
                t_arrived(which, 1 - core, n)

        cols = pl.ds(pl.multiple_of(last * cw + n * sw, sw), sw)
        w_cols = pl.ds(pl.multiple_of(n * sw, sw), sw)
        for b in range(acc.shape[0] // 256):
            rows = pl.ds(b * 256, 256)
            val = acc[rows, cols]
            for pos in (3, 7):
                val += jnp.dot(attn[rows, feature(pos)], wfull[units[pos], last, :, w_cols],
                               preferred_element_type=jnp.float32)
            acc[rows, cols] = val
            part[rows, :] += sum(val[:, k * 128:(k + 1) * 128] ** 2 for k in range(sw // 128))

    for b in range(part.shape[0] // 128):
        rows = slice(b * 128, (b + 1) * 128)
        sqbuf[0, :, rows] = jnp.sum(part[rows, :].T, axis=0, keepdims=True)
    x_sq = pltpu.make_async_remote_copy(
        src_ref=sqbuf.at[0], dst_ref=sqbuf.at[1], send_sem=x_send.at[0], recv_sem=x_recv.at[0],
        device_id=partner, device_id_type=MESH)
    x_sq.start()

    for pos in (5, 6):
        sent(SIB, pos, last)

    @pl.when(is_mid)
    def _():
        sent(ACROSS, 6, last)
        sent(SIB, 3, last)
        sent(SIB, 7, last)
        @pl.loop(0, CH)
        def _(j):
            sent(OUT, 6, j)

        for j in range(hc, last):
            sent(OUT, 1, j)
        for n in range(NS):
            t_out(n).wait_send()

    @pl.when(is_end)
    def _():
        for j in range(hc):
            sent(ACROSS, 2, j)
        for n in range(NS):
            t_across(n).wait_send()
            t_sib(0, n).wait_send()
            t_sib(1, n).wait_send()

    x_sq.wait()
    sq_ref[...] = sqbuf[0] + sqbuf[1]


NR = 128


def norm_kernel(acc, sq_ref, gain_ref, sum_ref, out_ref, hbuf, nbuf, hsem, nsem):
    rows = acc.shape[0]

    def copies(i):
        block = pl.ds(pl.multiple_of(i * NR, NR), NR)
        return (pltpu.make_async_copy(hbuf.at[block, :], sum_ref.at[block, :], hsem.at[i]),
                pltpu.make_async_copy(nbuf.at[block, :], out_ref.at[block, :], nsem.at[i]))

    @pl.loop(0, rows // NR)
    def _(i):
        block = pl.ds(pl.multiple_of(i * NR, NR), NR)
        scaled = lax.rsqrt(sq_ref[:, block] / D + jnp.float32(1e-05))
        column = jnp.broadcast_to(scaled, (128, NR)).T[:, :1]
        hid_copy, norm_copy = copies(i)
        for n in range(acc.shape[1] // 512):
            cols = slice(n * 512, (n + 1) * 512)
            hbuf[block, cols] = acc[block, cols].astype(jnp.bfloat16)
        hid_copy.start()
        for n in range(acc.shape[1] // 512):
            cols = slice(n * 512, (n + 1) * 512)
            nbuf[block, cols] = (acc[block, cols] * column * gain_ref[:, cols]).astype(jnp.bfloat16)
        norm_copy.start()

    @pl.loop(0, rows // NR)
    def _(i):
        for c in copies(i):
            c.wait()


def body_fused(query_proj, key_proj, value_proj, segment_ids, out_weight, residual, norm_gain):
    half, qw = query_proj.shape
    length = segment_ids.shape[1]
    wrows, width = out_weight.shape
    hbm = pl.BlockSpec(memory_space=pl.ANY)
    vmem = pl.BlockSpec(memory_space=pltpu.VMEM)
    dma = pltpu.SemaphoreType.DMA
    total, squares = pl.pallas_call(
        fused_kernel,
        out_shape=(
            pltpu.VMEM((length, width), jnp.float32),
            pltpu.VMEM((1, length), jnp.float32),
        ),
        in_specs=[hbm] * 6,
        out_specs=(vmem, vmem),
        scratch_shapes=[
            pltpu.VMEM((POS, CH, 2 * wrows, width // CH), jnp.bfloat16),
            pltpu.VMEM((2, length, HK * HD), jnp.bfloat16),
            pltpu.VMEM((half // QT, QT, KT), jnp.float32),
            pltpu.VMEM((length, qw), jnp.bfloat16),
            pltpu.VMEM((length, 128), jnp.float32),
            pltpu.VMEM((2, 1, length), jnp.float32),
            pltpu.VMEM((1, length), jnp.int32),
            dma((4, POS, CH)),
            dma((POS, 2, CH)),
            dma((4, NS)),
            dma((2, 2, NS)),
            dma((4,)),
            dma((CH,)),
            dma((2,)),
            dma((POS,)),
            dma((POS,)),
            dma((2, HK)),
            dma((2, HK)),
            dma((1,)),
            dma((1,)),
        ],
        compiler_params=pltpu.CompilerParams(
            collective_id=0, has_side_effects=True, vmem_limit_bytes=(47 * 1024 + 768) * 1024),
        name="fused",
    )(query_proj, key_proj, value_proj, segment_ids,
      out_weight, residual)
    total = pltpu.with_memory_space_constraint(total, pltpu.VMEM)
    squares = pltpu.with_memory_space_constraint(squares, pltpu.VMEM)
    return tuple(pl.pallas_call(
        norm_kernel,
        out_shape=(jax.ShapeDtypeStruct((length, width), jnp.bfloat16),) * 2,
        in_specs=[vmem, vmem, vmem],
        out_specs=(hbm, hbm),
        scratch_shapes=[
            pltpu.VMEM((length, width), jnp.bfloat16),
            pltpu.VMEM((length, width), jnp.bfloat16),
            dma((length // NR,)),
            dma((length // NR,)),
        ],
        compiler_params=pltpu.CompilerParams(vmem_limit_bytes=24 * 1024 * 1024),
        name="norm",
    )(total, squares, norm_gain.reshape(1, width)))


def solution(mesh):
    placed = (
        P(("col", "row"), None),
        P(("col", "row"), None),
        P(("col", "row"), None),
        P("col", None),
        P("col", "row"),
        P("col", "row"),
        P("row"),
    )
    known = mesh.shape["row"] == 2 and mesh.shape["col"] == 4 * NZ
    return jax.shard_map(
        body_fused if known else body_any,
        mesh=mesh,
        in_specs=placed,
        out_specs=(P("col", "row"), P("col", "row")),
        check_vma=False,
    )
```
